512 devices in a mesh: section: 8 (over z_hi, core), expert: 64 (over y, x, z_lo).
Axes of the slice: x: 4, y: 8, z: 8 (z_hi: 4, z_lo: 2; z = z_hi * 2 + z_lo), core: 2. Of those that a mesh axis runs over, the one named last changes fastest.
Arguments:
- tokens: bfloat16 [8, 16384, 1024], P('section', 'expert'), may hold values from -6 to 6
- gates: float32 [8, 16384], P('section', 'expert'), may hold values from 0.2 to 1
- routes: int32 [8, 16384, 1], P('section', 'expert'), may hold values from 0 to 63; in each aligned block of 256 rows (0 to 255, 256 to 511, ..., all dimensions but the last counted through in order) at most 8 rows name the same one
- capacity: int32 [8, 64], P('section', 'expert'), may hold values from 128 to 512
- mem_lengths: int32 [8, 64], P('section', 'expert'), may hold values from 64 to 256
- mem_keys: bfloat16 [8, 8192, 1024], P('section', 'expert')
- mem_values: bfloat16 [8, 8192, 1024], P('section', 'expert'), may hold values from -6 to 6
- q_weight: bfloat16 [8, 1024, 1024], P('section', 'expert'), may hold values from -0.1875 to 0.1875
- out_weight: bfloat16 [8, 1024, 1024], P('section', 'expert'), may hold values from -0.75 to 0.75
- w_in: bfloat16 [8, 64, 1024, 1408], P('section', 'expert'), may hold values from -0.1875 to 0.1875
Outputs:
- expert_hidden: bfloat16 [8, 16384, 1408], P('section', 'expert')
The draws below stay inside these ranges and needn't reach their ends.
Inputs may be any that keep to these rules, and one draw needn't show every extreme that they name: `routes`: among the 256 rows of one device at most 8 name one expert.
All inputs are finite; a program needn't handle non-finite values.
Results may differ from the reference program's by a relative error of at most 0.013.
Values may be sent and summed in bfloat16 or wider, within the bound.
No kernel may reach another device: no remote copies, remote signals or barrier semaphores. Data moves between devices by JAX's collectives and lax.ppermute only.
A program may use at most 64 MiB of HBM per device.

```python
import math
import jax
import jax.numpy as jnp
import numpy as np
from jax import lax

D = 1024
HEADS = 16
HEAD_DIM = 64
HID = 1408
TOK_DEV = 256
MEM_LEN = 256
MEM_HALF = 128
EXPERTS = 64
CAP_SRC = 8
TOKENS = 16384
MEM_ROWS = 8192
N_SECTION = 8
N_EXPERT = 64


def draw_mem_keys(key, part):
    first = jax.random.fold_in(key, 0)
    base = jax.random.normal(first, (N_SECTION, MEM_ROWS, D), jnp.float32)
    return base.astype(jnp.bfloat16)


def with_ends(result, stream_key, least, high):
    extent = result.shape
    index_at = [jax.random.randint(jax.random.fold_in(stream_key, axis), (), 0, extent[axis]) for axis in range(len(extent))]
    result = result.at[tuple(index_at)].set(least)
    longest = extent.index(max(extent))
    index_at[longest] = (index_at[longest] + 1) % extent[longest]
    return result.at[tuple(index_at)].set(high)


def block_levels(stream_key, extent, pieces, smallest, high):
    def one(dim, parts):
        heights = jax.random.uniform(jax.random.fold_in(jax.random.fold_in(stream_key, 6), dim), (parts,), jnp.float32, smallest / len(pieces), high / len(pieces))
        return jnp.repeat(jnp.exp(heights), extent[dim] // parts).reshape((-1,) + (1,) * (len(extent) - dim - 1))

    loudness = one(*pieces[0])
    for cut in pieces[1:]:
        loudness = loudness * one(*cut)
    return loudness


def assign_block(own_key, own, number, rows, number_of, top, bound, slope):
    order = jax.random.permutation(own_key, number_of)
    packed, ordinary = shares(number_of, rows * top, bound, slope, True), shares(number_of, rows * top, bound, slope, False)
    places = jnp.arange(number_of)

    def named(tallies, turn):
        used = int((tallies > 0).sum())
        fixed = max(1, used // 4)
        passed = fixed + (places - fixed + turn * (used - fixed)) % max(1, number_of - fixed)
        return jnp.zeros((number_of,), jnp.int32).at[order[jnp.where(places < fixed, places, passed)]].set(jnp.asarray(tallies, jnp.int32))

    tallies = jnp.where(number % 4 == 0, named(packed, number // 4), named(ordinary, number - number // 4 - 1))
    mixed = jax.random.permutation(jax.random.fold_in(own, 3), number_of)
    donor, taker = mixed[0:number_of // 2 * 2:2], mixed[1:number_of // 2 * 2:2]
    slack = jnp.minimum(tallies[donor] - 1, bound - tallies[taker]) // 2
    slack = jnp.where((donor == order[0]) | (taker == order[0]) | (tallies[taker] == 0), 0, jnp.maximum(slack, 0))
    passed = jax.random.randint(jax.random.fold_in(own, 4), (number_of // 2,), 0, 1 << 20) % (slack + 1)
    tallies = tallies.at[donor].add(-passed).at[taker].add(passed)
    labels = jnp.searchsorted(jnp.cumsum(tallies), jnp.arange(rows * top), side="right").astype(jnp.int32)
    table = labels.reshape(top, rows).T
    table = table[jax.random.permutation(jax.random.fold_in(own, 1), rows)]
    turn = jax.random.randint(jax.random.fold_in(own, 2), (rows, 1), 0, top)
    return jnp.take_along_axis(table, (jnp.arange(top)[None, :] + turn) % top, axis=1)


def shares(count, total, most, skew, full):
    portions = [(1 << 20) // math.isqrt(grade ** skew) + 1 for grade in range(1, count + 1)]
    largest = most if full else min(most, max(-(-total // count), total * portions[0] // sum(portions)))
    least = 1 if total - largest >= count - 1 else 0
    holding, rest = [largest] + [least] * (count - 1), total - largest - least * (count - 1)
    while rest > 0:
        free = [i for i in range(1, count) if holding[i] < largest] or [i for i in range(1, count) if holding[i] < most]
        pool, budget = sum([portions[i] for i in free]), rest
        for i in free:
            extra = min(most - holding[i], max(1, budget * portions[i] // pool), rest)
            holding[i] = holding[i] + extra
            rest = rest - extra
    return np.array(holding)


def bell_draw(stream_key, dims, spread, bound, cuts=(), kind=jnp.bfloat16):
    entries = spread * jax.random.normal(stream_key, dims, jnp.float32)
    if cuts:
        entries = entries * block_levels(stream_key, dims, cuts, -0.22, 0.18)
    return jnp.clip(entries, -bound, bound).astype(kind)


def setup_inputs(seed: int = 0) -> dict:
    arg_keys = jax.random.split(jax.random.key(seed), 11)
    tokens = bell_draw(arg_keys[0], (N_SECTION, TOKENS, D), 1.0, 6.0, ((0, 8), (1, 64)))
    gates = jnp.clip(jnp.exp(math.log(1.0) - 1.609438 * jax.random.uniform(arg_keys[1], (N_SECTION, TOKENS), jnp.float32) ** block_levels(arg_keys[1], (N_SECTION, TOKENS), ((0, 8), (1, 64)), -0.2, 0.2)), 0.2, 1.0)
    routes_keys = jax.random.split(jax.random.fold_in(arg_keys[2], 1), N_SECTION * TOKENS // TOK_DEV)
    routes_turns = jax.random.permutation(jax.random.fold_in(arg_keys[2], 3), N_SECTION * TOKENS // TOK_DEV)
    routes = jax.vmap(lambda own, number: assign_block(jax.random.fold_in(arg_keys[2], 2), own, number, TOK_DEV, EXPERTS, 1, CAP_SRC, 2))(routes_keys, routes_turns).reshape((N_SECTION, TOKENS, 1))
    capacity = with_ends(jax.random.randint(arg_keys[3], (N_SECTION, EXPERTS), TOK_DEV // 2, 2 * TOK_DEV + 1), jax.random.fold_in(arg_keys[3], 1), TOK_DEV // 2, 2 * TOK_DEV).astype(jnp.int32)
    mem_lengths = with_ends(jax.random.randint(arg_keys[4], (N_SECTION, N_EXPERT), MEM_LEN // 4, MEM_LEN + 1), jax.random.fold_in(arg_keys[4], 1), MEM_LEN // 4, MEM_LEN).astype(jnp.int32)
    mem_keys = draw_mem_keys(jax.random.fold_in(arg_keys[10], 71), 0)
    mem_values = bell_draw(arg_keys[6], (N_SECTION, MEM_ROWS, D), 1.0, 6.0, ((0, 8), (1, 64)))
    q_weight = bell_draw(arg_keys[7], (N_SECTION, D, D), D ** -0.5, 0.1875, ((0, 8), (1, 64)))
    out_weight = bell_draw(arg_keys[8], (N_SECTION, D, D), (D // 16) ** -0.5, 0.75, ((0, 8), (1, 64)))
    w_in = bell_draw(arg_keys[9], (N_SECTION, EXPERTS, D, HID), D ** -0.5, 0.1875, ((0, 8), (1, 64)))
    return {"tokens": tokens, "gates": gates, "routes": routes, "capacity": capacity, "mem_lengths": mem_lengths, "mem_keys": mem_keys, "mem_values": mem_values, "q_weight": q_weight, "out_weight": out_weight, "w_in": w_in}


def attend(query, keys, values, length):
    qh = query.reshape(TOK_DEV, HEADS, HEAD_DIM).astype(jnp.float32)
    kh = keys.reshape(MEM_LEN, HEADS, HEAD_DIM).astype(jnp.float32)
    vh = values.reshape(MEM_LEN, HEADS, HEAD_DIM).astype(jnp.float32)
    scores = jnp.einsum('qhd,khd->hqk', qh, kh) / jnp.sqrt(jnp.float32(HEAD_DIM))
    valid = jnp.arange(MEM_LEN, dtype=jnp.int32) < length
    scores = jnp.where(valid[None, None, :], scores, jnp.float32(-1e+30))
    scores = scores - lax.optimization_barrier(jnp.max(scores, axis=-1, keepdims=True))
    weights = jnp.exp(scores)
    probs = (weights / lax.optimization_barrier(jnp.sum(weights, axis=-1, keepdims=True))).astype(jnp.bfloat16)
    context = jnp.einsum('hqk,khd->qhd', probs.astype(jnp.float32), vh)
    return context.reshape(TOK_DEV, D).astype(jnp.bfloat16)

def reference(tokens, gates, routes, capacity, mem_lengths, mem_keys, mem_values, q_weight, out_weight, w_in):
    half = N_SECTION // 2
    results = []
    for section in range(N_SECTION):
        inputs = tokens[section]
        if section >= half:
            query = jnp.dot(inputs, q_weight[section], preferred_element_type=jnp.float32).astype(jnp.bfloat16)
            keys = jnp.concatenate([mem_keys[section - half].reshape(N_EXPERT, MEM_HALF, D), mem_keys[section].reshape(N_EXPERT, MEM_HALF, D)], axis=1)
            values = jnp.concatenate([mem_values[section - half].reshape(N_EXPERT, MEM_HALF, D), mem_values[section].reshape(N_EXPERT, MEM_HALF, D)], axis=1)
            context = lax.map(lambda item: attend(item[0], item[1], item[2], item[3]), (query.reshape(N_EXPERT, TOK_DEV, D), keys, values, mem_lengths[section]))
            context = context.reshape(TOKENS, D)
            attn_out = jnp.dot(context, out_weight[section], preferred_element_type=jnp.float32)
            mixed = (inputs.astype(jnp.float32) + attn_out).astype(jnp.bfloat16)
        else:
            mixed = inputs
        route = routes[section][:, 0].astype(jnp.int32)
        onehot = (route[:, None] == jnp.arange(EXPERTS, dtype=jnp.int32)[None, :]).astype(jnp.int32)
        grank = lax.optimization_barrier(jnp.sum((jnp.cumsum(onehot, axis=0) - onehot) * onehot, axis=1))
        kept = (grank < capacity[section][route]).astype(jnp.float32)
        local_hot = onehot.reshape(N_EXPERT, TOK_DEV, EXPERTS)
        lrank = lax.optimization_barrier(jnp.sum((jnp.cumsum(local_hot, axis=1) - local_hot) * local_hot, axis=2)).reshape(TOKENS)
        source = jnp.arange(TOKENS, dtype=jnp.int32) // TOK_DEV
        slot = (source * CAP_SRC + lrank).astype(jnp.int32)
        buffer = jnp.zeros((EXPERTS, N_EXPERT * CAP_SRC, D), jnp.bfloat16).at[route, slot].set(mixed)
        acts = lax.map(lambda item: jnp.maximum(jnp.dot(item[0], item[1], preferred_element_type=jnp.float32), 0.0).astype(jnp.bfloat16), (buffer, w_in[section]))
        picked = acts[route, slot].astype(jnp.float32)
        results.append((picked * gates[section][:, None] * kept[:, None]).astype(jnp.bfloat16))
    return jnp.stack(results, axis=0)
```

```python
import jax
import jax.numpy as jnp
from jax import lax
from jax.sharding import Mesh, PartitionSpec as P

HEADS = 16
EMPTY = 1e30
AXES = ("y", "x", "z")


def gathered(x, axis):
    peers = lax.axis_size(axis)
    return lax.all_to_all(jnp.broadcast_to(x[None], (peers, *x.shape)), axis, 0, 0, tiled=True)


def attend_block(query, keys, values, length):
    rows = query.shape[0]
    span = keys.shape[0]
    qh = query.reshape(rows, HEADS, -1)
    kh = keys.reshape(span, HEADS, -1)
    vh = values.reshape(span, HEADS, -1)
    scores = jnp.einsum("qhd,khd->hqk", qh, kh, preferred_element_type=jnp.float32) / jnp.sqrt(
        jnp.float32(qh.shape[2])
    )
    valid = jnp.arange(span, dtype=jnp.int32) < length
    scores = jnp.where(valid[None, None, :], scores, jnp.float32(-1e30))
    scores = scores - jnp.max(scores, axis=-1, keepdims=True)
    weights = jnp.exp(scores)
    probs = (weights / jnp.sum(weights, axis=-1, keepdims=True)).astype(jnp.bfloat16)
    context = jnp.einsum("hqk,khd->qhd", probs, vh, preferred_element_type=jnp.float32)
    return context.reshape(rows, -1).astype(jnp.bfloat16)


def shards(
    tokens, gates, routes, capacity, mem_lengths, mem_keys, mem_values, q_weight, out_weight, w_in
):
    sections = lax.axis_size("section")
    half = sections // 2
    experts = lax.axis_size(AXES)
    inputs = tokens[0]
    tok_dev, width = inputs.shape
    cap = max(8, 2 * tok_dev // experts)
    pairs = [(i, i + half) for i in range(half)]
    keys_far, values_far = lax.ppermute((mem_keys[0], mem_values[0]), "section", pairs)
    keys = jnp.concatenate([keys_far, mem_keys[0]], axis=0)
    values = jnp.concatenate([values_far, mem_values[0]], axis=0)

    both = jnp.stack([q_weight[0], out_weight[0]])
    both = gathered(gathered(both, "y"), ("x", "z"))
    both = both.transpose(2, 1, 0, 3, 4).reshape(2, width, width)
    wq, wo = both[0], both[1]

    query = jnp.dot(inputs, wq, preferred_element_type=jnp.float32).astype(jnp.bfloat16)
    context = attend_block(query, keys, values, mem_lengths[0, 0])
    attn_out = jnp.dot(context, wo, preferred_element_type=jnp.float32)
    decoding = lax.axis_index("section") >= half
    mixed = jnp.where(
        decoding, (inputs.astype(jnp.float32) + attn_out).astype(jnp.bfloat16), inputs
    )

    route = routes[0, :, 0]
    same = route[:, None] == route[None, :]
    earlier = jnp.arange(tok_dev)[None, :] < jnp.arange(tok_dev)[:, None]
    lrank = jnp.sum((same & earlier).astype(jnp.int32), axis=1)
    slot = route * cap + lrank
    placed = slot[:, None] == jnp.arange(experts * cap, dtype=jnp.int32)[None, :]
    placing = placed.astype(jnp.bfloat16)
    buffer = jnp.einsum("ts,td->sd", placing, mixed, preferred_element_type=jnp.float32).astype(
        jnp.bfloat16
    )
    used = jnp.any(placed, axis=0)
    buffer = jnp.where(used[:, None], buffer, jnp.bfloat16(EMPTY))
    received = lax.all_to_all(
        buffer.reshape(experts, cap, width), AXES, split_axis=0, concat_axis=0, tiled=True
    )
    filled = received[:, :, 0].astype(jnp.float32) < EMPTY / 2
    counts = jnp.sum(filled.astype(jnp.int32), axis=1)
    before = jnp.sum(
        jnp.where(jnp.arange(experts)[None, :] < jnp.arange(experts)[:, None], counts[None, :], 0),
        axis=1,
    )
    rank = before[:, None] + jnp.arange(cap, dtype=jnp.int32)[None, :]
    kept = filled & (rank < capacity[0, 0])
    acts = jnp.maximum(
        jnp.dot(
            received.reshape(experts * cap, width), w_in[0, 0], preferred_element_type=jnp.float32
        ),
        0.0,
    )
    acts = jnp.where(kept.reshape(-1)[:, None], acts, 0.0).astype(jnp.bfloat16)
    back = lax.all_to_all(
        acts.reshape(experts, cap, -1), AXES, split_axis=0, concat_axis=0, tiled=True
    )
    picked = jnp.dot(placing, back.reshape(experts * cap, -1), preferred_element_type=jnp.float32)
    result = (picked * gates[0][:, None]).astype(jnp.bfloat16)
    return result[None, :, :]


def solution(mesh):
    sections, experts = mesh.shape["section"], mesh.shape["expert"]
    x, z = 4, 2
    grid = Mesh(
        mesh.devices.reshape(sections, experts // (x * z), x, z), ("section", "y", "x", "z")
    )
    in_specs = (
        P("section", AXES, None),
        P("section", AXES),
        P("section", AXES, None),
        P("section", AXES),
        P("section", AXES),
        P("section", AXES, None),
        P("section", AXES, None),
        P("section", AXES, None),
        P("section", AXES, None),
        P("section", AXES, None, None),
    )
    out_specs = P("section", AXES, None)
    return jax.shard_map(shards, mesh=grid, in_specs=in_specs, out_specs=out_specs, check_vma=False)
```

```python
import jax
import jax.numpy as jnp
from jax import lax
from jax.sharding import Mesh, PartitionSpec as P

HEADS = 16
EMPTY = 1e30
AXES = ("y", "x", "z")


def gathered(x, axis):
    peers = lax.axis_size(axis)
    return lax.all_to_all(jnp.broadcast_to(x[None], (peers, *x.shape)), axis, 0, 0, tiled=True)


def attend_block(query, keys, values, length):
    rows = query.shape[0]
    span = keys.shape[0]
    qh = query.reshape(rows, HEADS, -1)
    kh = keys.reshape(span, HEADS, -1)
    vh = values.reshape(span, HEADS, -1)
    scores = jnp.einsum("qhd,khd->hqk", qh, kh, preferred_element_type=jnp.float32) / jnp.sqrt(
        jnp.float32(qh.shape[2])
    )
    valid = jnp.arange(span, dtype=jnp.int32) < length
    scores = jnp.where(valid[None, None, :], scores, jnp.float32(-1e30))
    scores = scores - jnp.max(scores, axis=-1, keepdims=True)
    weights = jnp.exp(scores)
    probs = (weights / jnp.sum(weights, axis=-1, keepdims=True)).astype(jnp.bfloat16)
    context = jnp.einsum("hqk,khd->qhd", probs, vh, preferred_element_type=jnp.float32)
    return context.reshape(rows, -1).astype(jnp.bfloat16)


def shards(
    tokens, gates, routes, capacity, mem_lengths, mem_keys, mem_values, q_weight, out_weight, w_in
):
    sections = lax.axis_size("section")
    half = sections // 2
    experts = lax.axis_size(AXES)
    inputs = tokens[0]
    tok_dev, width = inputs.shape
    cap = max(8, 2 * tok_dev // experts)
    pairs = [(i, i + half) for i in range(half)]
    keys_far, values_far = lax.ppermute((mem_keys[0], mem_values[0]), "section", pairs)
    spread = gathered(jnp.stack([q_weight[0], out_weight[0]]), "y")
    spread, keys_far, values_far = lax.optimization_barrier((spread, keys_far, values_far))
    keys = jnp.concatenate([keys_far, mem_keys[0]], axis=0)
    values = jnp.concatenate([values_far, mem_values[0]], axis=0)

    wq = gathered(spread[:, 0], ("x", "z"))
    wq, out_spread = lax.optimization_barrier((wq, spread[:, 1]))
    wo = gathered(out_spread, ("x", "z"))
    wq = wq.transpose(1, 0, 2, 3).reshape(width, width)
    wo = wo.transpose(1, 0, 2, 3).reshape(width, width)

    query = jnp.dot(inputs, wq, preferred_element_type=jnp.float32).astype(jnp.bfloat16)
    context = attend_block(query, keys, values, mem_lengths[0, 0])
    attn_out = jnp.dot(context, wo, preferred_element_type=jnp.float32)
    decoding = lax.axis_index("section") >= half
    mixed = jnp.where(
        decoding, (inputs.astype(jnp.float32) + attn_out).astype(jnp.bfloat16), inputs
    )

    route = routes[0, :, 0]
    same = route[:, None] == route[None, :]
    earlier = jnp.arange(tok_dev)[None, :] < jnp.arange(tok_dev)[:, None]
    lrank = jnp.sum((same & earlier).astype(jnp.int32), axis=1)
    slot = route * cap + lrank
    placed = slot[:, None] == jnp.arange(experts * cap, dtype=jnp.int32)[None, :]
    placing = placed.astype(jnp.bfloat16)
    buffer = jnp.einsum("ts,td->sd", placing, mixed, preferred_element_type=jnp.float32).astype(
        jnp.bfloat16
    )
    used = jnp.any(placed, axis=0)
    buffer = jnp.where(used[:, None], buffer, jnp.bfloat16(EMPTY))
    received = lax.all_to_all(
        buffer.reshape(experts, cap, width), AXES, split_axis=0, concat_axis=0, tiled=True
    )
    filled = received[:, :, 0].astype(jnp.float32) < EMPTY / 2
    counts = jnp.sum(filled.astype(jnp.int32), axis=1)
    before = jnp.sum(
        jnp.where(jnp.arange(experts)[None, :] < jnp.arange(experts)[:, None], counts[None, :], 0),
        axis=1,
    )
    rank = before[:, None] + jnp.arange(cap, dtype=jnp.int32)[None, :]
    kept = filled & (rank < capacity[0, 0])
    acts = jnp.maximum(
        jnp.dot(
            received.reshape(experts * cap, width), w_in[0, 0], preferred_element_type=jnp.float32
        ),
        0.0,
    )
    acts = jnp.where(kept.reshape(-1)[:, None], acts, 0.0).astype(jnp.bfloat16)
    back = lax.all_to_all(
        acts.reshape(experts, cap, -1), AXES, split_axis=0, concat_axis=0, tiled=True
    )
    picked = jnp.dot(placing, back.reshape(experts * cap, -1), preferred_element_type=jnp.float32)
    result = (picked * gates[0][:, None]).astype(jnp.bfloat16)
    return result[None, :, :]


def solution(mesh):
    sections, experts = mesh.shape["section"], mesh.shape["expert"]
    x, z = 4, 2
    grid = Mesh(
        mesh.devices.reshape(sections, experts // (x * z), x, z), ("section", "y", "x", "z")
    )
    in_specs = (
        P("section", AXES, None),
        P("section", AXES),
        P("section", AXES, None),
        P("section", AXES),
        P("section", AXES),
        P("section", AXES, None),
        P("section", AXES, None),
        P("section", AXES, None),
        P("section", AXES, None),
        P("section", AXES, None, None),
    )
    out_specs = P("section", AXES, None)
    return jax.shard_map(shards, mesh=grid, in_specs=in_specs, out_specs=out_specs, check_vma=False)
```

```python
import functools

import jax
import jax.numpy as jnp
from jax import lax
from jax.experimental import pallas as pl
from jax.experimental.pallas import tpu as pltpu
from jax.sharding import Mesh, PartitionSpec as P

HEADS = 16
EMPTY = 1e30
AXES = ("y", "x", "z")
VMEM = pl.BlockSpec(memory_space=pltpu.VMEM)
SMEM = pl.BlockSpec(memory_space=pltpu.SMEM)
PARAMS = pltpu.CompilerParams(vmem_limit_bytes=48 << 20)


def gathered(x, axis):
    peers = lax.axis_size(axis)
    return lax.all_to_all(jnp.broadcast_to(x[None], (peers, *x.shape)), axis, 0, 0, tiled=True)


def attend_block(query, keys, values, length):
    rows = query.shape[0]
    span = keys.shape[0]
    qh = query.reshape(rows, HEADS, -1)
    kh = keys.reshape(span, HEADS, -1)
    vh = values.reshape(span, HEADS, -1)
    scores = jnp.einsum("qhd,khd->hqk", qh, kh, preferred_element_type=jnp.float32) / jnp.sqrt(
        jnp.float32(qh.shape[2])
    )
    valid = jnp.arange(span, dtype=jnp.int32) < length
    scores = jnp.where(valid[None, None, :], scores, jnp.float32(-1e30))
    scores = scores - jnp.max(scores, axis=-1, keepdims=True)
    weights = jnp.exp(scores)
    probs = (weights / jnp.sum(weights, axis=-1, keepdims=True)).astype(jnp.bfloat16)
    context = jnp.einsum("hqk,khd->qhd", probs, vh, preferred_element_type=jnp.float32)
    return context.reshape(rows, -1).astype(jnp.bfloat16)


def mix_kernel(decoding, context, tokens, weight, slot, out):
    many, few, rows, width = weight.shape
    block = many * rows
    total = jnp.zeros((context.shape[0], width), jnp.float32)
    for k in range(few):
        piece = weight[:, k].reshape(block, width)
        total += jnp.dot(
            context[:, k * block : (k + 1) * block], piece, preferred_element_type=jnp.float32
        )
    own = tokens[...]
    added = (own.astype(jnp.float32) + total).astype(jnp.bfloat16)
    mixed = jnp.where(decoding[0] > 0, added, own)
    slots = out.shape[0]
    index = lax.broadcasted_iota(jnp.int32, (slots, own.shape[0]), 0)
    placed = (index == slot[...]).astype(jnp.float32)
    used = jnp.sum(placed, axis=1, keepdims=True) > 0.5
    sent = jnp.dot(placed.astype(jnp.bfloat16), mixed, preferred_element_type=jnp.float32)
    out[...] = jnp.where(used, sent, EMPTY).astype(jnp.bfloat16)


def expert_kernel(capacity, received, weight, out):
    rows = received.shape[0]
    filled = received[:, 0:128].astype(jnp.float32)[:, 0:1] < EMPTY / 2
    later = lax.broadcasted_iota(jnp.int32, (rows, rows), 0)
    sooner = lax.broadcasted_iota(jnp.int32, (rows, rows), 1)
    before = (sooner < later).astype(jnp.float32).astype(jnp.bfloat16)
    ones = jnp.where(jnp.broadcast_to(filled, (rows, 128)), 1.0, 0.0).astype(jnp.bfloat16)
    rank = jnp.dot(before, ones, preferred_element_type=jnp.float32)[:, 0:1]
    kept = filled & (rank < capacity[0].astype(jnp.float32))
    hidden = jnp.dot(received[...], weight[...], preferred_element_type=jnp.float32)
    out[...] = jnp.where(kept, jnp.maximum(hidden, 0.0), 0.0).astype(jnp.bfloat16)


def shards(
    tokens, gates, routes, capacity, mem_lengths, mem_keys, mem_values, q_weight, out_weight, w_in
):
    sections = lax.axis_size("section")
    half = sections // 2
    step = half // 2
    experts = lax.axis_size(AXES)
    inputs = tokens[0]
    tok_dev, width = inputs.shape
    cap = max(8, 2 * tok_dev // experts)

    ahead = functools.partial(lax.ppermute, axis_name="section")
    keys_far = ahead(mem_keys[0], perm=[(s, s + step) for s in range(half)])
    values_far = ahead(mem_values[0], perm=[(s, (s - step) % sections) for s in range(half)])

    spread = gathered(jnp.stack([q_weight[0], out_weight[0]]), "y")
    spread, keys_far, values_far = lax.optimization_barrier((spread, keys_far, values_far))

    keys_far = ahead(keys_far, perm=[(s, s + step) for s in range(step, half + step)])
    turned = [(s - step) % sections for s in range(half)]
    values_far = ahead(values_far, perm=[(s, (s - step) % sections) for s in turned])
    mine = spread[:, 0]
    other = lax.ppermute(mine, "z", [(0, 1), (1, 0)])
    wq_mine = gathered(mine, "x")
    wq_mine, other, keys_far, values_far, out_spread = lax.optimization_barrier(
        (wq_mine, other, keys_far, values_far, spread[:, 1])
    )
    wq_other = gathered(other, "x")
    wq_mine, wq_other, out_spread = lax.optimization_barrier((wq_mine, wq_other, out_spread))
    wo = gathered(out_spread, ("x", "z"))
    low = lax.axis_index("z") == 0
    wq = jnp.stack([jnp.where(low, wq_mine, wq_other), jnp.where(low, wq_other, wq_mine)])
    wq = wq.transpose(2, 1, 0, 3, 4).reshape(width, width)

    keys = jnp.concatenate([keys_far, mem_keys[0]], axis=0)
    values = jnp.concatenate([values_far, mem_values[0]], axis=0)
    query = jnp.dot(inputs, wq, preferred_element_type=jnp.float32).astype(jnp.bfloat16)
    context = attend_block(query, keys, values, mem_lengths[0, 0])

    route = routes[0, :, 0]
    same = route[:, None] == route[None, :]
    earlier = jnp.arange(tok_dev)[None, :] < jnp.arange(tok_dev)[:, None]
    lrank = jnp.sum((same & earlier).astype(jnp.int32), axis=1)
    slot = route * cap + lrank
    decoding = (lax.axis_index("section") >= half).astype(jnp.int32)

    buffer = pl.pallas_call(
        mix_kernel,
        out_shape=jax.ShapeDtypeStruct((experts * cap, width), jnp.bfloat16),
        in_specs=[SMEM, VMEM, VMEM, VMEM, VMEM],
        out_specs=VMEM,
        compiler_params=PARAMS,
        name="mix",
    )(decoding[None], context, inputs, wo, slot[None, :])
    received = lax.all_to_all(
        buffer.reshape(experts, cap, width), AXES, split_axis=0, concat_axis=0, tiled=True
    )
    acts = pl.pallas_call(
        expert_kernel,
        out_shape=jax.ShapeDtypeStruct((experts * cap, w_in.shape[-1]), jnp.bfloat16),
        in_specs=[SMEM, VMEM, VMEM],
        out_specs=VMEM,
        compiler_params=PARAMS,
        name="expert",
    )(capacity[0], received.reshape(experts * cap, width), w_in[0, 0])
    back = lax.all_to_all(
        acts.reshape(experts, cap, -1), AXES, split_axis=0, concat_axis=0, tiled=True
    )
    placing = (slot[:, None] == jnp.arange(experts * cap, dtype=jnp.int32)[None, :]).astype(
        jnp.bfloat16
    )
    picked = jnp.dot(placing, back.reshape(experts * cap, -1), preferred_element_type=jnp.float32)
    result = (picked * gates[0][:, None]).astype(jnp.bfloat16)
    return result[None, :, :]


def solution(mesh):
    sections, experts = mesh.shape["section"], mesh.shape["expert"]
    x, z = 4, 2
    grid = Mesh(
        mesh.devices.reshape(sections, experts // (x * z), x, z), ("section", "y", "x", "z")
    )
    in_specs = (
        P("section", AXES, None),
        P("section", AXES),
        P("section", AXES, None),
        P("section", AXES),
        P("section", AXES),
        P("section", AXES, None),
        P("section", AXES, None),
        P("section", AXES, None),
        P("section", AXES, None),
        P("section", AXES, None, None),
    )
    out_specs = P("section", AXES, None)
    return jax.shard_map(shards, mesh=grid, in_specs=in_specs, out_specs=out_specs, check_vma=False)
```

```python
import functools

import jax
import jax.numpy as jnp
from jax import lax
from jax.experimental import pallas as pl
from jax.experimental.pallas import tpu as pltpu
from jax.sharding import Mesh, PartitionSpec as P

HEADS = 16
EMPTY = 1e30
AXES = ("y", "x", "z")
VMEM = pl.BlockSpec(memory_space=pltpu.VMEM)
SMEM = pl.BlockSpec(memory_space=pltpu.SMEM)
PARAMS = pltpu.CompilerParams(vmem_limit_bytes=48 << 20)


def gathered(x, axis):
    peers = lax.axis_size(axis)
    return lax.all_to_all(jnp.broadcast_to(x[None], (peers, *x.shape)), axis, 0, 0, tiled=True)


def attend_block(query, keys, values, length):
    rows = query.shape[0]
    span = keys.shape[0]
    qh = query.reshape(rows, HEADS, -1)
    kh = keys.reshape(span, HEADS, -1)
    vh = values.reshape(span, HEADS, -1)
    scores = jnp.einsum("qhd,khd->hqk", qh, kh, preferred_element_type=jnp.float32) / jnp.sqrt(
        jnp.float32(qh.shape[2])
    )
    valid = jnp.arange(span, dtype=jnp.int32) < length
    scores = jnp.where(valid[None, None, :], scores, jnp.float32(-1e30))
    scores = scores - jnp.max(scores, axis=-1, keepdims=True)
    weights = jnp.exp(scores)
    probs = (weights / jnp.sum(weights, axis=-1, keepdims=True)).astype(jnp.bfloat16)
    context = jnp.einsum("hqk,khd->qhd", probs, vh, preferred_element_type=jnp.float32)
    return context.reshape(rows, -1).astype(jnp.bfloat16)


def mix_kernel(decoding, context, tokens, weight, slot, out):
    many, few, rows, width = weight.shape
    block = many * rows
    total = jnp.zeros((context.shape[0], width), jnp.float32)
    for k in range(few):
        piece = weight[:, k].reshape(block, width)
        total += jnp.dot(
            context[:, k * block : (k + 1) * block], piece, preferred_element_type=jnp.float32
        )
    own = tokens[...]
    added = (own.astype(jnp.float32) + total).astype(jnp.bfloat16)
    mixed = jnp.where(decoding[0] > 0, added, own)
    slots = out.shape[0]
    index = lax.broadcasted_iota(jnp.int32, (slots, own.shape[0]), 0)
    placed = (index == slot[...]).astype(jnp.float32)
    used = jnp.sum(placed, axis=1, keepdims=True) > 0.5
    sent = jnp.dot(placed.astype(jnp.bfloat16), mixed, preferred_element_type=jnp.float32)
    out[...] = jnp.where(used, sent, EMPTY).astype(jnp.bfloat16)


def expert_kernel(capacity, received, weight, out, held, sems):
    rows = received.shape[0]
    units = weight.shape[1]
    cuts = [0, units // 256 * 128, units]
    copies = []
    for k in range(2):
        part = slice(cuts[k], cuts[k + 1])
        copies.append(pltpu.make_async_copy(weight.at[:, part], held.at[:, part], sems.at[k]))
        copies[k].start()
    filled = received[:, 0:128].astype(jnp.float32)[:, 0:1] < EMPTY / 2
    later = lax.broadcasted_iota(jnp.int32, (rows, rows), 0)
    sooner = lax.broadcasted_iota(jnp.int32, (rows, rows), 1)
    before = (sooner < later).astype(jnp.float32).astype(jnp.bfloat16)
    ones = jnp.where(jnp.broadcast_to(filled, (rows, 128)), 1.0, 0.0).astype(jnp.bfloat16)
    rank = jnp.dot(before, ones, preferred_element_type=jnp.float32)[:, 0:1]
    kept = filled & (rank < capacity[0].astype(jnp.float32))
    for k in range(2):
        part = slice(cuts[k], cuts[k + 1])
        copies[k].wait()
        hidden = jnp.dot(received[...], held[:, part], preferred_element_type=jnp.float32)
        out[:, part] = jnp.where(kept, jnp.maximum(hidden, 0.0), 0.0).astype(jnp.bfloat16)


def shards(
    tokens, gates, routes, capacity, mem_lengths, mem_keys, mem_values, q_weight, out_weight, w_in
):
    sections = lax.axis_size("section")
    half = sections // 2
    step = half // 2
    experts = lax.axis_size(AXES)
    inputs = tokens[0]
    tok_dev, width = inputs.shape
    cap = max(8, 2 * tok_dev // experts)

    sides = lax.axis_size("z")
    over = [
        (s * sides + z, (s + half) * sides + (z + 1) % sides)
        for s in range(half)
        for z in range(sides)
    ]
    beside = [(z, (z + 1) % sides) for z in range(sides)]
    keys_far, values_far = lax.ppermute((mem_keys[0], mem_values[0]), ("section", "z"), over)

    spread = gathered(jnp.stack([q_weight[0], out_weight[0]]), "y")
    wq = gathered(spread[:, 0], ("x", "z"))
    wq, keys_far, values_far, out_spread = lax.optimization_barrier(
        (wq, keys_far, values_far, spread[:, 1])
    )
    wo = gathered(out_spread, ("x", "z"))
    keys_far, values_far = lax.ppermute((keys_far, values_far), "z", beside)
    wq = wq.transpose(1, 0, 2, 3).reshape(width, width)

    keys = jnp.concatenate([keys_far, mem_keys[0]], axis=0)
    values = jnp.concatenate([values_far, mem_values[0]], axis=0)
    query = jnp.dot(inputs, wq, preferred_element_type=jnp.float32).astype(jnp.bfloat16)
    context = attend_block(query, keys, values, mem_lengths[0, 0])

    route = routes[0, :, 0]
    same = route[:, None] == route[None, :]
    earlier = jnp.arange(tok_dev)[None, :] < jnp.arange(tok_dev)[:, None]
    lrank = jnp.sum((same & earlier).astype(jnp.int32), axis=1)
    slot = route * cap + lrank
    decoding = (lax.axis_index("section") >= half).astype(jnp.int32)

    buffer = pl.pallas_call(
        mix_kernel,
        out_shape=jax.ShapeDtypeStruct((experts * cap, width), jnp.bfloat16),
        in_specs=[SMEM, VMEM, VMEM, VMEM, VMEM],
        out_specs=VMEM,
        compiler_params=PARAMS,
        name="mix",
    )(decoding[None], context, inputs, wo, slot[None, :])
    received = lax.all_to_all(
        buffer.reshape(experts, cap, width), AXES, split_axis=0, concat_axis=0, tiled=True
    )
    acts = pl.pallas_call(
        expert_kernel,
        out_shape=jax.ShapeDtypeStruct((experts * cap, w_in.shape[-1]), jnp.bfloat16),
        in_specs=[SMEM, VMEM, pl.BlockSpec(memory_space=pltpu.HBM)],
        out_specs=VMEM,
        scratch_shapes=[
            pltpu.VMEM(w_in.shape[2:], jnp.bfloat16),
            pltpu.SemaphoreType.DMA((2,)),
        ],
        compiler_params=PARAMS,
        name="expert",
    )(capacity[0], received.reshape(experts * cap, width), w_in[0, 0])
    back = lax.all_to_all(
        acts.reshape(experts, cap, -1), AXES, split_axis=0, concat_axis=0, tiled=True
    )
    placing = (slot[:, None] == jnp.arange(experts * cap, dtype=jnp.int32)[None, :]).astype(
        jnp.bfloat16
    )
    picked = jnp.dot(placing, back.reshape(experts * cap, -1), preferred_element_type=jnp.float32)
    result = (picked * gates[0][:, None]).astype(jnp.bfloat16)
    return result[None, :, :]


def solution(mesh):
    sections, experts = mesh.shape["section"], mesh.shape["expert"]
    x, z = 4, 2
    grid = Mesh(
        mesh.devices.reshape(sections, experts // (x * z), x, z), ("section", "y", "x", "z")
    )
    in_specs = (
        P("section", AXES, None),
        P("section", AXES),
        P("section", AXES, None),
        P("section", AXES),
        P("section", AXES),
        P("section", AXES, None),
        P("section", AXES, None),
        P("section", AXES, None),
        P("section", AXES, None),
        P("section", AXES, None, None),
    )
    out_specs = P("section", AXES, None)
    return jax.shard_map(shards, mesh=grid, in_specs=in_specs, out_specs=out_specs, check_vma=False)
```

```python
import jax
import jax.numpy as jnp
from jax import lax
from jax.experimental import pallas as pl
from jax.experimental.pallas import tpu as pltpu
from jax.sharding import Mesh, PartitionSpec as P

HEADS = 16
EMPTY = 1e30
AXES = ("y", "x", "z")
VMEM = pl.BlockSpec(memory_space=pltpu.VMEM)
SMEM = pl.BlockSpec(memory_space=pltpu.SMEM)
PARAMS = pltpu.CompilerParams(vmem_limit_bytes=20 << 20)


def gathered(x, axis):
    peers = lax.axis_size(axis)
    return lax.all_to_all(jnp.broadcast_to(x[None], (peers, *x.shape)), axis, 0, 0, tiled=True)


def attend_block(query, keys, values, length):
    rows = query.shape[0]
    span = keys.shape[0]
    qh = query.reshape(rows, HEADS, -1)
    kh = keys.reshape(span, HEADS, -1)
    vh = values.reshape(span, HEADS, -1)
    scores = jnp.einsum("qhd,khd->hqk", qh, kh, preferred_element_type=jnp.float32) / jnp.sqrt(
        jnp.float32(qh.shape[2])
    )
    valid = jnp.arange(span, dtype=jnp.int32) < length
    scores = jnp.where(valid[None, None, :], scores, jnp.float32(-1e30))
    scores = scores - jnp.max(scores, axis=-1, keepdims=True)
    weights = jnp.exp(scores)
    probs = (weights / jnp.sum(weights, axis=-1, keepdims=True)).astype(jnp.bfloat16)
    context = jnp.einsum("hqk,khd->qhd", probs, vh, preferred_element_type=jnp.float32)
    return context.reshape(rows, -1).astype(jnp.bfloat16)


def mix_kernel(decoding, context, tokens, weight, slot, out):
    many, few, sides, rows, width = weight.shape
    block = many * sides * rows
    total = jnp.zeros((context.shape[0], width), jnp.float32)
    for k in range(few):
        piece = weight[:, k].reshape(block, width)
        total += jnp.dot(
            context[:, k * block : (k + 1) * block], piece, preferred_element_type=jnp.float32
        )
    own = tokens[...]
    added = (own.astype(jnp.float32) + total).astype(jnp.bfloat16)
    mixed = jnp.where(decoding[0] > 0, added, own)
    slots = out.shape[0]
    index = lax.broadcasted_iota(jnp.int32, (slots, own.shape[0]), 0)
    placed = (index == slot[...]).astype(jnp.float32)
    used = jnp.sum(placed, axis=1, keepdims=True) > 0.5
    sent = jnp.dot(placed.astype(jnp.bfloat16), mixed, preferred_element_type=jnp.float32)
    out[...] = jnp.where(used, sent, EMPTY).astype(jnp.bfloat16)


def expert_kernel(capacity, received, weight, out):
    rows = received.shape[0]
    filled = received[:, 0:128].astype(jnp.float32)[:, 0:1] < EMPTY / 2
    later = lax.broadcasted_iota(jnp.int32, (rows, rows), 0)
    sooner = lax.broadcasted_iota(jnp.int32, (rows, rows), 1)
    before = (sooner < later).astype(jnp.float32).astype(jnp.bfloat16)
    ones = jnp.where(jnp.broadcast_to(filled, (rows, 128)), 1.0, 0.0).astype(jnp.bfloat16)
    rank = jnp.dot(before, ones, preferred_element_type=jnp.float32)[:, 0:1]
    kept = filled & (rank < capacity[0].astype(jnp.float32))
    hidden = jnp.dot(received[...], weight[...], preferred_element_type=jnp.float32)
    out[...] = jnp.where(kept, jnp.maximum(hidden, 0.0), 0.0).astype(jnp.bfloat16)


def shards(
    tokens, gates, routes, capacity, mem_lengths, mem_keys, mem_values, q_weight, out_weight, w_in
):
    sections = lax.axis_size("section")
    half = sections // 2
    step = half // 2
    experts = lax.axis_size(AXES)
    inputs = tokens[0]
    tok_dev, width = inputs.shape
    cap = max(8, 2 * tok_dev // experts)

    across = [(s, s + half) for s in range(half)]
    keys_far = lax.ppermute(mem_keys[0], "section", across)
    values_far = lax.ppermute(mem_values[0], "section", across)

    mine = jnp.stack([q_weight[0], out_weight[0]])
    other = lax.ppermute(mine, "z", [(0, 1), (1, 0)])
    low = lax.axis_index("z") == 0
    spread = jnp.stack([jnp.where(low, mine, other), jnp.where(low, other, mine)], axis=1)
    spread = gathered(spread, "y")
    spread, keys_far = lax.optimization_barrier((spread, keys_far))
    wq = gathered(spread[:, 0], "x")
    wq, values_far, out_spread = lax.optimization_barrier((wq, values_far, spread[:, 1]))
    wo = gathered(out_spread, "x")
    wq = wq.transpose(1, 0, 2, 3, 4).reshape(width, width)

    keys = jnp.concatenate([keys_far, mem_keys[0]], axis=0)
    values = jnp.concatenate([values_far, mem_values[0]], axis=0)
    query = jnp.dot(inputs, wq, preferred_element_type=jnp.float32).astype(jnp.bfloat16)
    context = attend_block(query, keys, values, mem_lengths[0, 0])

    route = routes[0, :, 0]
    same = route[:, None] == route[None, :]
    earlier = jnp.arange(tok_dev)[None, :] < jnp.arange(tok_dev)[:, None]
    lrank = jnp.sum((same & earlier).astype(jnp.int32), axis=1)
    slot = route * cap + lrank
    decoding = (lax.axis_index("section") >= half).astype(jnp.int32)

    buffer = pl.pallas_call(
        mix_kernel,
        out_shape=jax.ShapeDtypeStruct((experts * cap, width), jnp.bfloat16),
        in_specs=[SMEM, VMEM, VMEM, VMEM, VMEM],
        out_specs=VMEM,
        compiler_params=PARAMS,
        name="mix",
    )(decoding[None], context, inputs, wo, slot[None, :])
    received = lax.all_to_all(
        buffer.reshape(experts, cap, width), AXES, split_axis=0, concat_axis=0, tiled=True
    )
    acts = pl.pallas_call(
        expert_kernel,
        out_shape=jax.ShapeDtypeStruct((experts * cap, w_in.shape[-1]), jnp.bfloat16),
        in_specs=[SMEM, VMEM, VMEM],
        out_specs=VMEM,
        compiler_params=PARAMS,
        name="expert",
    )(capacity[0], received.reshape(experts * cap, width), w_in[0, 0])
    back = lax.all_to_all(
        acts.reshape(experts, cap, -1), AXES, split_axis=0, concat_axis=0, tiled=True
    )
    placing = (slot[:, None] == jnp.arange(experts * cap, dtype=jnp.int32)[None, :]).astype(
        jnp.bfloat16
    )
    picked = jnp.dot(placing, back.reshape(experts * cap, -1), preferred_element_type=jnp.float32)
    result = (picked * gates[0][:, None]).astype(jnp.bfloat16)
    return result[None, :, :]


def solution(mesh):
    sections, experts = mesh.shape["section"], mesh.shape["expert"]
    x, z = 4, 2
    grid = Mesh(
        mesh.devices.reshape(sections, experts // (x * z), x, z), ("section", "y", "x", "z")
    )
    in_specs = (
        P("section", AXES, None),
        P("section", AXES),
        P("section", AXES, None),
        P("section", AXES),
        P("section", AXES),
        P("section", AXES, None),
        P("section", AXES, None),
        P("section", AXES, None),
        P("section", AXES, None),
        P("section", AXES, None, None),
    )
    out_specs = P("section", AXES, None)
    return jax.shard_map(shards, mesh=grid, in_specs=in_specs, out_specs=out_specs, check_vma=False)
```

```python
import jax
import jax.numpy as jnp
from jax import lax
from jax.experimental import pallas as pl
from jax.experimental.pallas import tpu as pltpu
from jax.sharding import Mesh, PartitionSpec as P

HEADS = 16
EMPTY = 1e30
AXES = ("y", "x", "z")
VMEM = pl.BlockSpec(memory_space=pltpu.VMEM)
SMEM = pl.BlockSpec(memory_space=pltpu.SMEM)
PARAMS = pltpu.CompilerParams(vmem_limit_bytes=20 << 20)


def gathered(x, axis):
    peers = lax.axis_size(axis)
    return lax.all_to_all(jnp.broadcast_to(x[None], (peers, *x.shape)), axis, 0, 0, tiled=True)


def whole(mine, other, low, which):
    first = jnp.where(low, mine[:, :, which], other[:, :, which])
    second = jnp.where(low, other[:, :, which], mine[:, :, which])
    both = jnp.stack([first, second], axis=2)
    return jnp.swapaxes(both, 0, 1).reshape(-1, mine.shape[-1])


def decode_kernel(
    facts, tokens, keys_far, keys_near, values_far, values_near, mine, other, slot, out, query, context
):
    decoding, length, low = facts[0] > 0, facts[1], facts[2] > 0
    own = tokens[...]
    rows, width = own.shape
    slab = 128
    dim = width // HEADS
    query[...] = jnp.dot(
        own, whole(mine, other, low, 0), preferred_element_type=jnp.float32
    ).astype(jnp.bfloat16)
    span = keys_far.shape[0] + keys_near.shape[0]
    valid = lax.broadcasted_iota(jnp.int32, (rows, span), 1) < length
    lane = lax.broadcasted_iota(jnp.int32, (rows, slab), 1)
    for p in range(width // slab):
        part = slice(p * slab, (p + 1) * slab)
        keys = jnp.concatenate([keys_far[:, part], keys_near[:, part]], axis=0)
        values = jnp.concatenate([values_far[:, part], values_near[:, part]], axis=0)
        pair = query[:, part]
        found = jnp.zeros((rows, slab), jnp.float32)
        for h in range(slab // dim):
            here = (lane >= h * dim) & (lane < (h + 1) * dim)
            asked = jnp.where(here, pair, jnp.zeros_like(pair))
            scores = lax.dot_general(
                asked, keys, (((1,), (1,)), ((), ())), preferred_element_type=jnp.float32
            ) * (dim**-0.5)
            scores = jnp.where(valid, scores, -1e30)
            weights = jnp.exp(scores - jnp.max(scores, axis=1, keepdims=True))
            probs = weights * (1.0 / jnp.sum(weights, axis=1, keepdims=True))
            seen = jnp.dot(probs.astype(jnp.bfloat16), values, preferred_element_type=jnp.float32)
            found = jnp.where(here, seen, found)
        context[:, part] = found.astype(jnp.bfloat16)
    total = jnp.dot(
        context[...], whole(mine, other, low, 1), preferred_element_type=jnp.float32
    )
    added = (own.astype(jnp.float32) + total).astype(jnp.bfloat16)
    mixed = jnp.where(decoding, added, own)
    slots = out.shape[0]
    index = lax.broadcasted_iota(jnp.int32, (slots, rows), 0)
    placed = (index == slot[...]).astype(jnp.float32)
    used = jnp.sum(placed, axis=1, keepdims=True) > 0.5
    sent = jnp.dot(placed.astype(jnp.bfloat16), mixed, preferred_element_type=jnp.float32)
    out[...] = jnp.where(used, sent, EMPTY).astype(jnp.bfloat16)


def expert_kernel(capacity, received, weight, out, held, sems):
    rows = received.shape[0]
    units = weight.shape[1]
    cuts = [0, units // 256 * 128, units]
    copies = []
    for k in range(2):
        part = slice(cuts[k], cuts[k + 1])
        copies.append(pltpu.make_async_copy(weight.at[:, part], held.at[:, part], sems.at[k]))
        copies[k].start()
    filled = received[:, 0:128].astype(jnp.float32)[:, 0:1] < EMPTY / 2
    later = lax.broadcasted_iota(jnp.int32, (rows, rows), 0)
    sooner = lax.broadcasted_iota(jnp.int32, (rows, rows), 1)
    before = (sooner < later).astype(jnp.float32).astype(jnp.bfloat16)
    ones = jnp.where(jnp.broadcast_to(filled, (rows, 128)), 1.0, 0.0).astype(jnp.bfloat16)
    rank = jnp.dot(before, ones, preferred_element_type=jnp.float32)[:, 0:1]
    kept = filled & (rank < capacity[0].astype(jnp.float32))
    for k in range(2):
        part = slice(cuts[k], cuts[k + 1])
        copies[k].wait()
        hidden = jnp.dot(received[...], held[:, part], preferred_element_type=jnp.float32)
        out[:, part] = jnp.where(kept, jnp.maximum(hidden, 0.0), 0.0).astype(jnp.bfloat16)


def shards(
    tokens, gates, routes, capacity, mem_lengths, mem_keys, mem_values, q_weight, out_weight, w_in
):
    sections = lax.axis_size("section")
    half = sections // 2
    step = half // 2
    experts = lax.axis_size(AXES)
    inputs = tokens[0]
    tok_dev, width = inputs.shape
    cap = max(8, 2 * tok_dev // experts)

    across = [(s, s + half) for s in range(half)]
    keys_far = lax.ppermute(mem_keys[0], "section", across)
    values_far = lax.ppermute(mem_values[0], "section", across)

    spread = gathered(jnp.stack([q_weight[0], out_weight[0]]), "y")
    beside = lax.ppermute(spread, "z", [(0, 1), (1, 0)])
    mine = gathered(spread, "x")
    mine, beside, keys_far = lax.optimization_barrier((mine, beside, keys_far))
    other = gathered(beside, "x")
    mine, other, values_far = lax.optimization_barrier((mine, other, values_far))

    route = routes[0, :, 0]
    same = route[:, None] == route[None, :]
    earlier = jnp.arange(tok_dev)[None, :] < jnp.arange(tok_dev)[:, None]
    lrank = jnp.sum((same & earlier).astype(jnp.int32), axis=1)
    slot = route * cap + lrank
    decoding = (lax.axis_index("section") >= half).astype(jnp.int32)

    low = (lax.axis_index("z") == 0).astype(jnp.int32)
    facts = jnp.stack([decoding, mem_lengths[0, 0], low])
    buffer = pl.pallas_call(
        decode_kernel,
        out_shape=jax.ShapeDtypeStruct((experts * cap, width), jnp.bfloat16),
        in_specs=[SMEM] + [VMEM] * 8,
        out_specs=VMEM,
        scratch_shapes=[pltpu.VMEM((tok_dev, width), jnp.bfloat16)] * 2,
        compiler_params=pltpu.CompilerParams(vmem_limit_bytes=32 << 20),
        name="decode",
    )(
        facts,
        inputs,
        keys_far,
        mem_keys[0],
        values_far,
        mem_values[0],
        mine,
        other,
        slot[None, :],
    )
    received = lax.all_to_all(
        buffer.reshape(experts, cap, width), AXES, split_axis=0, concat_axis=0, tiled=True
    )
    acts = pl.pallas_call(
        expert_kernel,
        out_shape=jax.ShapeDtypeStruct((experts * cap, w_in.shape[-1]), jnp.bfloat16),
        in_specs=[SMEM, VMEM, pl.BlockSpec(memory_space=pltpu.HBM)],
        out_specs=VMEM,
        scratch_shapes=[
            pltpu.VMEM(w_in.shape[2:], jnp.bfloat16),
            pltpu.SemaphoreType.DMA((2,)),
        ],
        compiler_params=PARAMS,
        name="expert",
    )(
        capacity[0],
        received.reshape(experts * cap, width),
        pltpu.with_memory_space_constraint(w_in[0, 0], pltpu.HBM),
    )
    back = lax.all_to_all(
        acts.reshape(experts, cap, -1), AXES, split_axis=0, concat_axis=0, tiled=True
    )
    placing = (slot[:, None] == jnp.arange(experts * cap, dtype=jnp.int32)[None, :]).astype(
        jnp.bfloat16
    )
    picked = jnp.dot(placing, back.reshape(experts * cap, -1), preferred_element_type=jnp.float32)
    result = (picked * gates[0][:, None]).astype(jnp.bfloat16)
    return result[None, :, :]


def solution(mesh):
    sections, experts = mesh.shape["section"], mesh.shape["expert"]
    x, z = 4, 2
    grid = Mesh(
        mesh.devices.reshape(sections, experts // (x * z), x, z), ("section", "y", "x", "z")
    )
    in_specs = (
        P("section", AXES, None),
        P("section", AXES),
        P("section", AXES, None),
        P("section", AXES),
        P("section", AXES),
        P("section", AXES, None),
        P("section", AXES, None),
        P("section", AXES, None),
        P("section", AXES, None),
        P("section", AXES, None, None),
    )
    out_specs = P("section", AXES, None)
    return jax.shard_map(shards, mesh=grid, in_specs=in_specs, out_specs=out_specs, check_vma=False)
```

```python
import jax
import jax.numpy as jnp
from jax import lax
from jax.experimental import pallas as pl
from jax.experimental.pallas import tpu as pltpu
from jax.sharding import Mesh, PartitionSpec as P

HEADS = 16
EMPTY = 1e30
AXES = ("y", "x", "z")
VMEM = pl.BlockSpec(memory_space=pltpu.VMEM)
SMEM = pl.BlockSpec(memory_space=pltpu.SMEM)
PARAMS = pltpu.CompilerParams(vmem_limit_bytes=20 << 20)


def widened(x, axis):
    return jnp.broadcast_to(x[None], (lax.axis_size(axis), *x.shape))


def gathered(x, axis):
    return lax.all_to_all(widened(x, axis), axis, 0, 0, tiled=True)


def whole(mine, other, low, which):
    first = jnp.where(low, mine[:, :, which], other[:, :, which])
    second = jnp.where(low, other[:, :, which], mine[:, :, which])
    both = jnp.stack([first, second], axis=2)
    return jnp.swapaxes(both, 0, 1).reshape(-1, mine.shape[-1])


def decode_kernel(
    facts, tokens, keys_far, keys_near, values_far, values_near, mine, other, slot, out, query, context
):
    decoding, length, low = facts[0] > 0, facts[1], facts[2] > 0
    own = tokens[...]
    rows, width = own.shape
    slab = 128
    dim = width // HEADS
    query[...] = jnp.dot(
        own, whole(mine, other, low, 0), preferred_element_type=jnp.float32
    ).astype(jnp.bfloat16)
    span = keys_far.shape[0] + keys_near.shape[0]
    valid = lax.broadcasted_iota(jnp.int32, (rows, span), 1) < length
    lane = lax.broadcasted_iota(jnp.int32, (rows, slab), 1)
    for p in range(width // slab):
        part = slice(p * slab, (p + 1) * slab)
        keys = jnp.concatenate([keys_far[:, part], keys_near[:, part]], axis=0)
        values = jnp.concatenate([values_far[:, part], values_near[:, part]], axis=0)
        pair = query[:, part]
        found = jnp.zeros((rows, slab), jnp.float32)
        for h in range(slab // dim):
            here = (lane >= h * dim) & (lane < (h + 1) * dim)
            asked = jnp.where(here, pair, jnp.zeros_like(pair))
            scores = lax.dot_general(
                asked, keys, (((1,), (1,)), ((), ())), preferred_element_type=jnp.float32
            ) * (dim**-0.5)
            scores = jnp.where(valid, scores, -1e30)
            weights = jnp.exp(scores - jnp.max(scores, axis=1, keepdims=True))
            probs = weights * (1.0 / jnp.sum(weights, axis=1, keepdims=True))
            seen = jnp.dot(probs.astype(jnp.bfloat16), values, preferred_element_type=jnp.float32)
            found = jnp.where(here, seen, found)
        context[:, part] = found.astype(jnp.bfloat16)
    total = jnp.dot(
        context[...], whole(mine, other, low, 1), preferred_element_type=jnp.float32
    )
    added = (own.astype(jnp.float32) + total).astype(jnp.bfloat16)
    mixed = jnp.where(decoding, added, own)
    slots = out.shape[0]
    index = lax.broadcasted_iota(jnp.int32, (slots, rows), 0)
    placed = (index == slot[...]).astype(jnp.float32)
    used = jnp.sum(placed, axis=1, keepdims=True) > 0.5
    sent = jnp.dot(placed.astype(jnp.bfloat16), mixed, preferred_element_type=jnp.float32)
    out[...] = jnp.where(used, sent, EMPTY).astype(jnp.bfloat16)


def fetch_kernel(stored, held, sem):
    copy = pltpu.make_async_copy(stored, held, sem)
    copy.start()
    copy.wait()


def expert_kernel(capacity, received, weight, out):
    rows = received.shape[0]
    filled = received[:, 0:128].astype(jnp.float32)[:, 0:1] < EMPTY / 2
    later = lax.broadcasted_iota(jnp.int32, (rows, rows), 0)
    sooner = lax.broadcasted_iota(jnp.int32, (rows, rows), 1)
    before = (sooner < later).astype(jnp.float32).astype(jnp.bfloat16)
    ones = jnp.where(jnp.broadcast_to(filled, (rows, 128)), 1.0, 0.0).astype(jnp.bfloat16)
    rank = jnp.dot(before, ones, preferred_element_type=jnp.float32)[:, 0:1]
    kept = filled & (rank < capacity[0].astype(jnp.float32))
    hidden = jnp.dot(received[...], weight[...], preferred_element_type=jnp.float32)
    out[...] = jnp.where(kept, jnp.maximum(hidden, 0.0), 0.0).astype(jnp.bfloat16)


def shards(
    tokens, gates, routes, capacity, mem_lengths, mem_keys, mem_values, q_weight, out_weight, w_in
):
    sections = lax.axis_size("section")
    half = sections // 2
    step = half // 2
    experts = lax.axis_size(AXES)
    inputs = tokens[0]
    tok_dev, width = inputs.shape
    cap = max(8, 2 * tok_dev // experts)

    across = [(s, s + half) for s in range(half)]
    keys_far = lax.ppermute(mem_keys[0], "section", across)
    values_far = lax.ppermute(mem_values[0], "section", across)

    spread = gathered(jnp.stack([q_weight[0], out_weight[0]]), "y")
    spread, keys_far = lax.optimization_barrier((spread, keys_far))
    beside = lax.ppermute(spread, "z", [(0, 1), (1, 0)])
    mine = gathered(spread, "x")
    beside = widened(beside, "x")
    mine, beside, values_far = lax.optimization_barrier((mine, beside, values_far))
    other = lax.all_to_all(beside, "x", 0, 0, tiled=True)

    route = routes[0, :, 0]
    same = route[:, None] == route[None, :]
    earlier = jnp.arange(tok_dev)[None, :] < jnp.arange(tok_dev)[:, None]
    lrank = jnp.sum((same & earlier).astype(jnp.int32), axis=1)
    slot = route * cap + lrank
    decoding = (lax.axis_index("section") >= half).astype(jnp.int32)

    low = (lax.axis_index("z") == 0).astype(jnp.int32)
    facts = jnp.stack([decoding, mem_lengths[0, 0], low])
    buffer = pl.pallas_call(
        decode_kernel,
        out_shape=jax.ShapeDtypeStruct((experts * cap, width), jnp.bfloat16),
        in_specs=[SMEM] + [VMEM] * 8,
        out_specs=VMEM,
        scratch_shapes=[pltpu.VMEM((tok_dev, width), jnp.bfloat16)] * 2,
        compiler_params=pltpu.CompilerParams(vmem_limit_bytes=32 << 20),
        name="decode",
    )(
        facts,
        inputs,
        keys_far,
        mem_keys[0],
        values_far,
        mem_values[0],
        mine,
        other,
        slot[None, :],
    )
    received = lax.all_to_all(
        buffer.reshape(experts, cap, width), AXES, split_axis=0, concat_axis=0, tiled=True
    )
    hidden_weight = pl.pallas_call(
        fetch_kernel,
        out_shape=jax.ShapeDtypeStruct(w_in.shape[2:], jnp.bfloat16),
        in_specs=[pl.BlockSpec(memory_space=pltpu.HBM)],
        out_specs=VMEM,
        scratch_shapes=[pltpu.SemaphoreType.DMA(())],
        compiler_params=PARAMS,
        name="fetch",
    )(pltpu.with_memory_space_constraint(w_in[0, 0], pltpu.HBM))
    acts = pl.pallas_call(
        expert_kernel,
        out_shape=jax.ShapeDtypeStruct((experts * cap, w_in.shape[-1]), jnp.bfloat16),
        in_specs=[SMEM, VMEM, VMEM],
        out_specs=VMEM,
        compiler_params=PARAMS,
        name="expert",
    )(capacity[0], received.reshape(experts * cap, width), hidden_weight)
    back = lax.all_to_all(
        acts.reshape(experts, cap, -1), AXES, split_axis=0, concat_axis=0, tiled=True
    )
    placing = (slot[:, None] == jnp.arange(experts * cap, dtype=jnp.int32)[None, :]).astype(
        jnp.bfloat16
    )
    picked = jnp.dot(placing, back.reshape(experts * cap, -1), preferred_element_type=jnp.float32)
    result = (picked * gates[0][:, None]).astype(jnp.bfloat16)
    return result[None, :, :]


def solution(mesh):
    sections, experts = mesh.shape["section"], mesh.shape["expert"]
    x, z = 4, 2
    grid = Mesh(
        mesh.devices.reshape(sections, experts // (x * z), x, z), ("section", "y", "x", "z")
    )
    in_specs = (
        P("section", AXES, None),
        P("section", AXES),
        P("section", AXES, None),
        P("section", AXES),
        P("section", AXES),
        P("section", AXES, None),
        P("section", AXES, None),
        P("section", AXES, None),
        P("section", AXES, None),
        P("section", AXES, None, None),
    )
    out_specs = P("section", AXES, None)
    return jax.shard_map(shards, mesh=grid, in_specs=in_specs, out_specs=out_specs, check_vma=False)
```

```python
import jax
import jax.numpy as jnp
from jax import lax
from jax.experimental import pallas as pl
from jax.experimental.pallas import tpu as pltpu
from jax.sharding import Mesh, PartitionSpec as P

HEADS = 16
EMPTY = 1e30
AXES = ("y", "x", "z")
VMEM = pl.BlockSpec(memory_space=pltpu.VMEM)
SMEM = pl.BlockSpec(memory_space=pltpu.SMEM)
PARAMS = pltpu.CompilerParams(vmem_limit_bytes=20 << 20)
SMALL = pltpu.CompilerParams(vmem_limit_bytes=4 << 20)


def widen_kernel(x, out, sems):
    copies = [pltpu.make_async_copy(x, out.at[i], sems.at[i]) for i in range(out.shape[0])]
    for copy in copies:
        copy.start()
    for copy in copies:
        copy.wait()


def widened(x, axis):
    peers = lax.axis_size(axis)
    return pl.pallas_call(
        widen_kernel,
        out_shape=jax.ShapeDtypeStruct((peers, *x.shape), x.dtype),
        in_specs=[pl.BlockSpec(memory_space=pl.ANY)],
        out_specs=pl.BlockSpec(memory_space=pltpu.HBM),
        scratch_shapes=[pltpu.SemaphoreType.DMA((peers,))],
        compiler_params=SMALL,
        name="widen",
    )(x)


def gathered(x, axis):
    return lax.all_to_all(widened(x, axis), axis, 0, 0, tiled=True)


def whole(mine, other, low, which):
    first = jnp.where(low, mine[:, :, which], other[:, :, which])
    second = jnp.where(low, other[:, :, which], mine[:, :, which])
    both = jnp.stack([first, second], axis=2)
    return jnp.swapaxes(both, 0, 1).reshape(-1, mine.shape[-1])


def decode_kernel(
    facts, tokens, keys_far, keys_near, values_far, values_near, mine, other, slot, out, query, context
):
    decoding, length, low = facts[0] > 0, facts[1], facts[2] > 0
    own = tokens[...]
    rows, width = own.shape
    slab = 128
    dim = width // HEADS
    query[...] = jnp.dot(
        own, whole(mine, other, low, 0), preferred_element_type=jnp.float32
    ).astype(jnp.bfloat16)
    span = keys_far.shape[0] + keys_near.shape[0]
    valid = lax.broadcasted_iota(jnp.int32, (rows, span), 1) < length
    lane = lax.broadcasted_iota(jnp.int32, (rows, slab), 1)
    lane_all = lax.broadcasted_iota(jnp.int32, (span, slab), 1)
    here_all = [(lane_all >= h * dim) & (lane_all < (h + 1) * dim) for h in range(slab // dim)]
    for p in range(width // slab):
        part = slice(p * slab, (p + 1) * slab)
        keys = jnp.concatenate([keys_far[:, part], keys_near[:, part]], axis=0)
        values = jnp.concatenate([values_far[:, part], values_near[:, part]], axis=0)
        pair = query[:, part]
        found = jnp.zeros((rows, slab), jnp.float32)
        for h in range(slab // dim):
            here = (lane >= h * dim) & (lane < (h + 1) * dim)
            asked = jnp.where(here, pair, jnp.zeros_like(pair))
            scores = lax.dot_general(
                asked, keys, (((1,), (1,)), ((), ())), preferred_element_type=jnp.float32
            ) * (dim**-0.5)
            scores = jnp.where(valid, scores, -1e30)
            weights = jnp.exp(scores - jnp.max(scores, axis=1, keepdims=True))
            columns = jnp.where(here_all[h], values, jnp.ones_like(values))
            seen = jnp.dot(weights.astype(jnp.bfloat16), columns, preferred_element_type=jnp.float32)
            sums = pltpu.roll(seen, dim, 1)
            found = jnp.where(here, seen / sums, found)
        context[:, part] = found.astype(jnp.bfloat16)
    total = jnp.dot(
        context[...], whole(mine, other, low, 1), preferred_element_type=jnp.float32
    )
    added = (own.astype(jnp.float32) + total).astype(jnp.bfloat16)
    mixed = jnp.where(decoding, added, own)
    slots = out.shape[0]
    index = lax.broadcasted_iota(jnp.int32, (slots, rows), 0)
    placed = (index == slot[...]).astype(jnp.float32)
    used = jnp.sum(placed, axis=1, keepdims=True) > 0.5
    sent = jnp.dot(placed.astype(jnp.bfloat16), mixed, preferred_element_type=jnp.float32)
    out[...] = jnp.where(used, sent, EMPTY).astype(jnp.bfloat16)


def fetch_kernel(stored, held, sem):
    copy = pltpu.make_async_copy(stored.at[:, 0 : held.shape[1]], held, sem)
    copy.start()
    copy.wait()


def expert_kernel(capacity, received, first, stored, out, rest, acts, sems):
    rows, units = acts.shape
    cut = first.shape[1]
    loading = pltpu.make_async_copy(stored.at[:, cut:units], rest, sems.at[0])
    loading.start()
    filled = received[:, 0:128].astype(jnp.float32)[:, 0:1] < EMPTY / 2
    later = lax.broadcasted_iota(jnp.int32, (rows, rows), 0)
    sooner = lax.broadcasted_iota(jnp.int32, (rows, rows), 1)
    before = (sooner < later).astype(jnp.float32).astype(jnp.bfloat16)
    ones = jnp.where(jnp.broadcast_to(filled, (rows, 128)), 1.0, 0.0).astype(jnp.bfloat16)
    rank = jnp.dot(before, ones, preferred_element_type=jnp.float32)[:, 0:1]
    kept = filled & (rank < capacity[0].astype(jnp.float32))
    storing = []
    for k, weight in enumerate((first, rest)):
        part = slice(k * cut, k * cut + weight.shape[1])
        if k == 1:
            loading.wait()
        hidden = jnp.dot(received[...], weight[...], preferred_element_type=jnp.float32)
        acts[:, part] = jnp.where(kept, jnp.maximum(hidden, 0.0), 0.0).astype(jnp.bfloat16)
        storing.append(pltpu.make_async_copy(acts.at[:, part], out.at[:, part], sems.at[1 + k]))
        storing[k].start()
    for copy in storing:
        copy.wait()


def shards(
    tokens, gates, routes, capacity, mem_lengths, mem_keys, mem_values, q_weight, out_weight, w_in
):
    sections = lax.axis_size("section")
    half = sections // 2
    step = half // 2
    experts = lax.axis_size(AXES)
    inputs = tokens[0]
    tok_dev, width = inputs.shape
    cap = max(8, 2 * tok_dev // experts)

    across = [(s, s + half) for s in range(half)]
    keys_far = lax.ppermute(mem_keys[0], "section", across)
    values_far = lax.ppermute(mem_values[0], "section", across)

    spread = gathered(jnp.stack([q_weight[0], out_weight[0]]), "y")
    beside = lax.ppermute(spread, "z", [(0, 1), (1, 0)])
    mine = gathered(spread, "x")
    mine, beside, keys_far = lax.optimization_barrier((mine, beside, keys_far))
    other = gathered(beside, "x")
    mine, other, values_far = lax.optimization_barrier((mine, other, values_far))

    route = routes[0, :, 0]
    same = route[:, None] == route[None, :]
    earlier = jnp.arange(tok_dev)[None, :] < jnp.arange(tok_dev)[:, None]
    lrank = jnp.sum((same & earlier).astype(jnp.int32), axis=1)
    slot = route * cap + lrank
    decoding = (lax.axis_index("section") >= half).astype(jnp.int32)

    low = (lax.axis_index("z") == 0).astype(jnp.int32)
    facts = jnp.stack([decoding, mem_lengths[0, 0], low])
    buffer = pl.pallas_call(
        decode_kernel,
        out_shape=jax.ShapeDtypeStruct((experts * cap, width), jnp.bfloat16),
        in_specs=[SMEM] + [VMEM] * 8,
        out_specs=VMEM,
        scratch_shapes=[pltpu.VMEM((tok_dev, width), jnp.bfloat16)] * 2,
        compiler_params=pltpu.CompilerParams(vmem_limit_bytes=32 << 20),
        name="decode",
    )(
        facts,
        inputs,
        keys_far,
        mem_keys[0],
        values_far,
        mem_values[0],
        mine,
        other,
        slot[None, :],
    )
    received = lax.all_to_all(
        buffer.reshape(experts, cap, width), AXES, split_axis=0, concat_axis=0, tiled=True
    )
    units = w_in.shape[-1]
    cut = units // 256 * 128
    stored = pltpu.with_memory_space_constraint(w_in[0, 0], pltpu.HBM)
    first = pl.pallas_call(
        fetch_kernel,
        out_shape=jax.ShapeDtypeStruct((width, cut), jnp.bfloat16),
        in_specs=[pl.BlockSpec(memory_space=pltpu.HBM)],
        out_specs=VMEM,
        scratch_shapes=[pltpu.SemaphoreType.DMA(())],
        compiler_params=SMALL,
        name="fetch",
    )(stored)
    acts = pl.pallas_call(
        expert_kernel,
        out_shape=pltpu.HBM((experts * cap, units), jnp.bfloat16),
        in_specs=[SMEM, VMEM, VMEM, pl.BlockSpec(memory_space=pltpu.HBM)],
        out_specs=pl.BlockSpec(memory_space=pltpu.HBM),
        scratch_shapes=[
            pltpu.VMEM((width, units - cut), jnp.bfloat16),
            pltpu.VMEM((experts * cap, units), jnp.bfloat16),
            pltpu.SemaphoreType.DMA((3,)),
        ],
        compiler_params=PARAMS,
        name="expert",
    )(capacity[0], received.reshape(experts * cap, width), first, stored)
    back = lax.all_to_all(
        acts.reshape(experts, cap, -1), AXES, split_axis=0, concat_axis=0, tiled=True
    )
    placing = (slot[:, None] == jnp.arange(experts * cap, dtype=jnp.int32)[None, :]).astype(
        jnp.bfloat16
    )
    picked = jnp.dot(placing, back.reshape(experts * cap, -1), preferred_element_type=jnp.float32)
    result = (picked * gates[0][:, None]).astype(jnp.bfloat16)
    return result[None, :, :]


def solution(mesh):
    sections, experts = mesh.shape["section"], mesh.shape["expert"]
    x, z = 4, 2
    grid = Mesh(
        mesh.devices.reshape(sections, experts // (x * z), x, z), ("section", "y", "x", "z")
    )
    in_specs = (
        P("section", AXES, None),
        P("section", AXES),
        P("section", AXES, None),
        P("section", AXES),
        P("section", AXES),
        P("section", AXES, None),
        P("section", AXES, None),
        P("section", AXES, None),
        P("section", AXES, None),
        P("section", AXES, None, None),
    )
    out_specs = P("section", AXES, None)
    return jax.shard_map(shards, mesh=grid, in_specs=in_specs, out_specs=out_specs, check_vma=False)
```

```python
import jax
import jax.numpy as jnp
from jax import lax
from jax.experimental import pallas as pl
from jax.experimental.pallas import tpu as pltpu
from jax.sharding import Mesh, PartitionSpec as P

HEADS = 16
EMPTY = 1e30
AXES = ("y", "x", "z")
VMEM = pl.BlockSpec(memory_space=pltpu.VMEM)
SMEM = pl.BlockSpec(memory_space=pltpu.SMEM)
PARAMS = pltpu.CompilerParams(vmem_limit_bytes=20 << 20)
SMALL = pltpu.CompilerParams(vmem_limit_bytes=4 << 20)


def widen_kernel(*refs):
    *pieces, out, sems = refs
    copies = []
    for i in range(out.shape[0]):
        for k, piece in enumerate(pieces):
            to = out.at[i, k] if len(pieces) > 1 else out.at[i]
            copies.append(pltpu.make_async_copy(piece, to, sems.at[i, k]))
    for copy in copies:
        copy.start()
    for copy in copies:
        copy.wait()


def gathered(pieces, axis):
    peers, first = lax.axis_size(axis), pieces[0]
    inner = (len(pieces), *first.shape) if len(pieces) > 1 else first.shape
    wide = pl.pallas_call(
        widen_kernel,
        out_shape=jax.ShapeDtypeStruct((peers, *inner), first.dtype),
        in_specs=[pl.BlockSpec(memory_space=pl.ANY)] * len(pieces),
        out_specs=pl.BlockSpec(memory_space=pltpu.HBM),
        scratch_shapes=[pltpu.SemaphoreType.DMA((peers, len(pieces)))],
        compiler_params=SMALL,
        name="widen",
    )(*pieces)
    return lax.all_to_all(wide, axis, 0, 0, tiled=True)


def whole(mine, other, low, which):
    first = jnp.where(low, mine[:, :, which], other[:, :, which])
    second = jnp.where(low, other[:, :, which], mine[:, :, which])
    both = jnp.stack([first, second], axis=2)
    return jnp.swapaxes(both, 0, 1).reshape(-1, mine.shape[-1])


def decode_kernel(
    facts, tokens, keys_far, keys_near, values_far, values_near, mine, other, slot, out, query, context
):
    decoding, length, low = facts[0] > 0, facts[1], facts[2] > 0
    own = tokens[...]
    rows, width = own.shape
    slab = 128
    dim = width // HEADS
    query[...] = jnp.dot(
        own, whole(mine, other, low, 0), preferred_element_type=jnp.float32
    ).astype(jnp.bfloat16)
    span = keys_far.shape[0] + keys_near.shape[0]
    valid = lax.broadcasted_iota(jnp.int32, (rows, span), 1) < length
    lane = lax.broadcasted_iota(jnp.int32, (rows, slab), 1)
    for p in range(width // slab):
        part = slice(p * slab, (p + 1) * slab)
        keys = jnp.concatenate([keys_far[:, part], keys_near[:, part]], axis=0)
        values = jnp.concatenate([values_far[:, part], values_near[:, part]], axis=0)
        pair = query[:, part]
        found = jnp.zeros((rows, slab), jnp.float32)
        for h in range(slab // dim):
            here = (lane >= h * dim) & (lane < (h + 1) * dim)
            asked = jnp.where(here, pair, jnp.zeros_like(pair))
            scores = lax.dot_general(
                asked, keys, (((1,), (1,)), ((), ())), preferred_element_type=jnp.float32
            ) * (dim**-0.5)
            scores = jnp.where(valid, scores, -1e30)
            weights = jnp.exp(scores - jnp.max(scores, axis=1, keepdims=True))
            probs = weights * (1.0 / jnp.sum(weights, axis=1, keepdims=True))
            seen = jnp.dot(probs.astype(jnp.bfloat16), values, preferred_element_type=jnp.float32)
            found = jnp.where(here, seen, found)
        context[:, part] = found.astype(jnp.bfloat16)
    total = jnp.dot(
        context[...], whole(mine, other, low, 1), preferred_element_type=jnp.float32
    )
    added = (own.astype(jnp.float32) + total).astype(jnp.bfloat16)
    mixed = jnp.where(decoding, added, own)
    slots = out.shape[0]
    index = lax.broadcasted_iota(jnp.int32, (slots, rows), 0)
    placed = (index == slot[...]).astype(jnp.float32)
    used = jnp.sum(placed, axis=1, keepdims=True) > 0.5
    sent = jnp.dot(placed.astype(jnp.bfloat16), mixed, preferred_element_type=jnp.float32)
    out[...] = jnp.where(used, sent, EMPTY).astype(jnp.bfloat16)


def fetch_kernel(stored, held, sem):
    copy = pltpu.make_async_copy(stored.at[:, 0 : held.shape[1]], held, sem)
    copy.start()
    copy.wait()


def expert_kernel(capacity, received, first, stored, out, rest, acts, sems):
    rows, units = acts.shape
    cut = first.shape[1]
    loading = pltpu.make_async_copy(stored.at[:, cut:units], rest, sems.at[0])
    loading.start()
    filled = received[:, 0:128].astype(jnp.float32)[:, 0:1] < EMPTY / 2
    later = lax.broadcasted_iota(jnp.int32, (rows, rows), 0)
    sooner = lax.broadcasted_iota(jnp.int32, (rows, rows), 1)
    before = (sooner < later).astype(jnp.float32).astype(jnp.bfloat16)
    ones = jnp.where(jnp.broadcast_to(filled, (rows, 128)), 1.0, 0.0).astype(jnp.bfloat16)
    rank = jnp.dot(before, ones, preferred_element_type=jnp.float32)[:, 0:1]
    kept = filled & (rank < capacity[0].astype(jnp.float32))
    middle = cut // 256 * 128
    parts = [(0, first, 0, middle), (0, first, middle, cut), (cut, rest, 0, units - cut)]
    storing = []
    for k, (base, weight, low, high) in enumerate(parts):
        part = slice(base + low, base + high)
        if weight is rest:
            loading.wait()
        hidden = jnp.dot(received[...], weight[:, low:high], preferred_element_type=jnp.float32)
        acts[:, part] = jnp.where(kept, jnp.maximum(hidden, 0.0), 0.0).astype(jnp.bfloat16)
        storing.append(pltpu.make_async_copy(acts.at[:, part], out.at[:, part], sems.at[1 + k]))
        storing[k].start()
    for copy in storing:
        copy.wait()


def shards(
    tokens, gates, routes, capacity, mem_lengths, mem_keys, mem_values, q_weight, out_weight, w_in
):
    sections = lax.axis_size("section")
    half = sections // 2
    step = half // 2
    experts = lax.axis_size(AXES)
    inputs = tokens[0]
    tok_dev, width = inputs.shape
    cap = max(8, 2 * tok_dev // experts)

    across = [(s, s + half) for s in range(half)]
    keys_far = lax.ppermute(mem_keys[0], "section", across)
    values_far = lax.ppermute(mem_values[0], "section", across)

    spread = gathered([q_weight[0], out_weight[0]], "y")
    beside = lax.ppermute(spread, "z", [(0, 1), (1, 0)])
    mine = gathered([spread], "x")
    mine, beside, keys_far = lax.optimization_barrier((mine, beside, keys_far))
    other = gathered([beside], "x")
    mine, other, values_far = lax.optimization_barrier((mine, other, values_far))

    route = routes[0, :, 0]
    same = route[:, None] == route[None, :]
    earlier = jnp.arange(tok_dev)[None, :] < jnp.arange(tok_dev)[:, None]
    lrank = jnp.sum((same & earlier).astype(jnp.int32), axis=1)
    slot = route * cap + lrank
    decoding = (lax.axis_index("section") >= half).astype(jnp.int32)

    low = (lax.axis_index("z") == 0).astype(jnp.int32)
    facts = jnp.stack([decoding, mem_lengths[0, 0], low])
    buffer = pl.pallas_call(
        decode_kernel,
        out_shape=jax.ShapeDtypeStruct((experts * cap, width), jnp.bfloat16),
        in_specs=[SMEM] + [VMEM] * 8,
        out_specs=VMEM,
        scratch_shapes=[pltpu.VMEM((tok_dev, width), jnp.bfloat16)] * 2,
        compiler_params=pltpu.CompilerParams(vmem_limit_bytes=32 << 20),
        name="decode",
    )(
        facts,
        inputs,
        keys_far,
        mem_keys[0],
        values_far,
        mem_values[0],
        mine,
        other,
        slot[None, :],
    )
    received = lax.all_to_all(
        buffer.reshape(experts, cap, width), AXES, split_axis=0, concat_axis=0, tiled=True
    )
    units = w_in.shape[-1]
    cut = units // 512 * 512
    stored = pltpu.with_memory_space_constraint(w_in[0, 0], pltpu.HBM)
    first = pl.pallas_call(
        fetch_kernel,
        out_shape=jax.ShapeDtypeStruct((width, cut), jnp.bfloat16),
        in_specs=[pl.BlockSpec(memory_space=pltpu.HBM)],
        out_specs=VMEM,
        scratch_shapes=[pltpu.SemaphoreType.DMA(())],
        compiler_params=SMALL,
        name="fetch",
    )(stored)
    acts = pl.pallas_call(
        expert_kernel,
        out_shape=pltpu.HBM((experts * cap, units), jnp.bfloat16),
        in_specs=[SMEM, VMEM, VMEM, pl.BlockSpec(memory_space=pltpu.HBM)],
        out_specs=pl.BlockSpec(memory_space=pltpu.HBM),
        scratch_shapes=[
            pltpu.VMEM((width, units - cut), jnp.bfloat16),
            pltpu.VMEM((experts * cap, units), jnp.bfloat16),
            pltpu.SemaphoreType.DMA((4,)),
        ],
        compiler_params=PARAMS,
        name="expert",
    )(capacity[0], received.reshape(experts * cap, width), first, stored)
    back = lax.all_to_all(
        acts.reshape(experts, cap, -1), AXES, split_axis=0, concat_axis=0, tiled=True
    )
    placing = (slot[:, None] == jnp.arange(experts * cap, dtype=jnp.int32)[None, :]).astype(
        jnp.bfloat16
    )
    picked = jnp.dot(placing, back.reshape(experts * cap, -1), preferred_element_type=jnp.float32)
    result = (picked * gates[0][:, None]).astype(jnp.bfloat16)
    return result[None, :, :]


def solution(mesh):
    sections, experts = mesh.shape["section"], mesh.shape["expert"]
    x, z = 4, 2
    grid = Mesh(
        mesh.devices.reshape(sections, experts // (x * z), x, z), ("section", "y", "x", "z")
    )
    in_specs = (
        P("section", AXES, None),
        P("section", AXES),
        P("section", AXES, None),
        P("section", AXES),
        P("section", AXES),
        P("section", AXES, None),
        P("section", AXES, None),
        P("section", AXES, None),
        P("section", AXES, None),
        P("section", AXES, None, None),
    )
    out_specs = P("section", AXES, None)
    return jax.shard_map(shards, mesh=grid, in_specs=in_specs, out_specs=out_specs, check_vma=False)
```

```python
import jax
import jax.numpy as jnp
from jax import lax
from jax.experimental import pallas as pl
from jax.experimental.pallas import tpu as pltpu
from jax.sharding import Mesh, PartitionSpec as P

HEADS = 16
EMPTY = 1e30
AXES = ("y", "x", "z")
VMEM = pl.BlockSpec(memory_space=pltpu.VMEM)
SMEM = pl.BlockSpec(memory_space=pltpu.SMEM)
PARAMS = pltpu.CompilerParams(vmem_limit_bytes=20 << 20)
SMALL = pltpu.CompilerParams(vmem_limit_bytes=4 << 20)


def widen_kernel(*refs):
    *pieces, out, sems = refs
    copies = []
    for i in range(out.shape[0]):
        for k, piece in enumerate(pieces):
            to = out.at[i, k] if len(pieces) > 1 else out.at[i]
            copies.append(pltpu.make_async_copy(piece, to, sems.at[i, k]))
    for copy in copies:
        copy.start()
    for copy in copies:
        copy.wait()


def widened(pieces, axis):
    peers, first = lax.axis_size(axis), pieces[0]
    inner = (len(pieces), *first.shape) if len(pieces) > 1 else first.shape
    return pl.pallas_call(
        widen_kernel,
        out_shape=jax.ShapeDtypeStruct((peers, *inner), first.dtype),
        in_specs=[pl.BlockSpec(memory_space=pl.ANY)] * len(pieces),
        out_specs=pl.BlockSpec(memory_space=pltpu.HBM),
        scratch_shapes=[pltpu.SemaphoreType.DMA((peers, len(pieces)))],
        compiler_params=SMALL,
        cost_estimate=pl.CostEstimate(
            flops=0, transcendentals=0, bytes_accessed=4 * peers * len(pieces) * first.size
        ),
        name="widen",
    )(*pieces)


def gathered(pieces, axis):
    return lax.all_to_all(widened(pieces, axis), axis, 0, 0, tiled=True)


def whole(mine, other, low, which):
    first = jnp.where(low, mine[:, :, which], other[:, :, which])
    second = jnp.where(low, other[:, :, which], mine[:, :, which])
    both = jnp.stack([first, second], axis=2)
    return jnp.swapaxes(both, 0, 1).reshape(-1, mine.shape[-1])


def decode_kernel(
    facts, tokens, keys_far, keys_near, values_far, values_near, mine, other, slot, out, query, context
):
    decoding, length, low = facts[0] > 0, facts[1], facts[2] > 0
    own = tokens[...]
    rows, width = own.shape
    slab = 128
    dim = width // HEADS
    query[...] = jnp.dot(
        own, whole(mine, other, low, 0), preferred_element_type=jnp.float32
    ).astype(jnp.bfloat16)
    span = keys_far.shape[0] + keys_near.shape[0]
    valid = lax.broadcasted_iota(jnp.int32, (rows, span), 1) < length
    lane = lax.broadcasted_iota(jnp.int32, (rows, slab), 1)
    for p in range(width // slab):
        part = slice(p * slab, (p + 1) * slab)
        keys = jnp.concatenate([keys_far[:, part], keys_near[:, part]], axis=0)
        values = jnp.concatenate([values_far[:, part], values_near[:, part]], axis=0)
        pair = query[:, part]
        found = jnp.zeros((rows, slab), jnp.float32)
        for h in range(slab // dim):
            here = (lane >= h * dim) & (lane < (h + 1) * dim)
            asked = jnp.where(here, pair, jnp.zeros_like(pair))
            scores = lax.dot_general(
                asked, keys, (((1,), (1,)), ((), ())), preferred_element_type=jnp.float32
            ) * (dim**-0.5)
            scores = jnp.where(valid, scores, -1e30)
            weights = jnp.exp(scores - jnp.max(scores, axis=1, keepdims=True))
            probs = weights * (1.0 / jnp.sum(weights, axis=1, keepdims=True))
            seen = jnp.dot(probs.astype(jnp.bfloat16), values, preferred_element_type=jnp.float32)
            found = jnp.where(here, seen, found)
        context[:, part] = found.astype(jnp.bfloat16)
    total = jnp.dot(
        context[...], whole(mine, other, low, 1), preferred_element_type=jnp.float32
    )
    added = (own.astype(jnp.float32) + total).astype(jnp.bfloat16)
    mixed = jnp.where(decoding, added, own)
    slots = out.shape[0]
    index = lax.broadcasted_iota(jnp.int32, (slots, rows), 0)
    placed = (index == slot[...]).astype(jnp.float32)
    used = jnp.sum(placed, axis=1, keepdims=True) > 0.5
    sent = jnp.dot(placed.astype(jnp.bfloat16), mixed, preferred_element_type=jnp.float32)
    out[...] = jnp.where(used, sent, EMPTY).astype(jnp.bfloat16)


def fetch_kernel(stored, held, sem):
    copy = pltpu.make_async_copy(stored.at[:, 0 : held.shape[1]], held, sem)
    copy.start()
    copy.wait()


def expert_kernel(capacity, received, first, stored, out, rest, acts, sems):
    rows, units = acts.shape
    cut = first.shape[1]
    loading = pltpu.make_async_copy(stored.at[:, cut:units], rest, sems.at[0])
    loading.start()
    filled = received[:, 0:128].astype(jnp.float32)[:, 0:1] < EMPTY / 2
    later = lax.broadcasted_iota(jnp.int32, (rows, rows), 0)
    sooner = lax.broadcasted_iota(jnp.int32, (rows, rows), 1)
    before = (sooner < later).astype(jnp.float32).astype(jnp.bfloat16)
    ones = jnp.where(jnp.broadcast_to(filled, (rows, 128)), 1.0, 0.0).astype(jnp.bfloat16)
    rank = jnp.dot(before, ones, preferred_element_type=jnp.float32)[:, 0:1]
    kept = filled & (rank < capacity[0].astype(jnp.float32))
    middle = cut // 256 * 128
    parts = [(0, first, 0, middle), (0, first, middle, cut), (cut, rest, 0, units - cut)]
    storing = []
    for k, (base, weight, low, high) in enumerate(parts):
        part = slice(base + low, base + high)
        if weight is rest:
            loading.wait()
        hidden = jnp.dot(received[...], weight[:, low:high], preferred_element_type=jnp.float32)
        acts[:, part] = jnp.where(kept, jnp.maximum(hidden, 0.0), 0.0).astype(jnp.bfloat16)
        storing.append(pltpu.make_async_copy(acts.at[:, part], out.at[:, part], sems.at[1 + k]))
        storing[k].start()
    for copy in storing:
        copy.wait()


def shards(
    tokens, gates, routes, capacity, mem_lengths, mem_keys, mem_values, q_weight, out_weight, w_in
):
    sections = lax.axis_size("section")
    half = sections // 2
    step = half // 2
    experts = lax.axis_size(AXES)
    inputs = tokens[0]
    tok_dev, width = inputs.shape
    cap = max(8, 2 * tok_dev // experts)

    across = [(s, s + half) for s in range(half)]
    keys_far = lax.ppermute(mem_keys[0], "section", across)
    values_far = lax.ppermute(mem_values[0], "section", across)

    spread = gathered(
        [pltpu.with_memory_space_constraint(w[0], pltpu.HBM) for w in (q_weight, out_weight)], "y"
    )
    beside = lax.ppermute(spread, "z", [(0, 1), (1, 0)])
    beside = widened([beside], "x")
    mine = gathered([spread], "x")
    mine, beside, keys_far = lax.optimization_barrier((mine, beside, keys_far))
    other = lax.all_to_all(beside, "x", 0, 0, tiled=True)
    mine, other, values_far = lax.optimization_barrier((mine, other, values_far))

    route = routes[0, :, 0]
    same = route[:, None] == route[None, :]
    earlier = jnp.arange(tok_dev)[None, :] < jnp.arange(tok_dev)[:, None]
    lrank = jnp.sum((same & earlier).astype(jnp.int32), axis=1)
    slot = route * cap + lrank
    decoding = (lax.axis_index("section") >= half).astype(jnp.int32)

    low = (lax.axis_index("z") == 0).astype(jnp.int32)
    facts = jnp.stack([decoding, mem_lengths[0, 0], low])
    buffer = pl.pallas_call(
        decode_kernel,
        out_shape=jax.ShapeDtypeStruct((experts * cap, width), jnp.bfloat16),
        in_specs=[SMEM] + [VMEM] * 8,
        out_specs=VMEM,
        scratch_shapes=[pltpu.VMEM((tok_dev, width), jnp.bfloat16)] * 2,
        compiler_params=pltpu.CompilerParams(vmem_limit_bytes=32 << 20),
        name="decode",
    )(
        facts,
        inputs,
        keys_far,
        mem_keys[0],
        values_far,
        mem_values[0],
        mine,
        other,
        slot[None, :],
    )
    received = lax.all_to_all(
        buffer.reshape(experts, cap, width), AXES, split_axis=0, concat_axis=0, tiled=True
    )
    units = w_in.shape[-1]
    cut = units // 512 * 512
    stored = pltpu.with_memory_space_constraint(w_in[0, 0], pltpu.HBM)
    first = pl.pallas_call(
        fetch_kernel,
        out_shape=jax.ShapeDtypeStruct((width, cut), jnp.bfloat16),
        in_specs=[pl.BlockSpec(memory_space=pltpu.HBM)],
        out_specs=VMEM,
        scratch_shapes=[pltpu.SemaphoreType.DMA(())],
        compiler_params=SMALL,
        name="fetch",
    )(stored)
    acts = pl.pallas_call(
        expert_kernel,
        out_shape=pltpu.HBM((experts * cap, units), jnp.bfloat16),
        in_specs=[SMEM, VMEM, VMEM, pl.BlockSpec(memory_space=pltpu.HBM)],
        out_specs=pl.BlockSpec(memory_space=pltpu.HBM),
        scratch_shapes=[
            pltpu.VMEM((width, units - cut), jnp.bfloat16),
            pltpu.VMEM((experts * cap, units), jnp.bfloat16),
            pltpu.SemaphoreType.DMA((4,)),
        ],
        compiler_params=PARAMS,
        name="expert",
    )(capacity[0], received.reshape(experts * cap, width), first, stored)
    back = lax.all_to_all(
        acts.reshape(experts, cap, -1), AXES, split_axis=0, concat_axis=0, tiled=True
    )
    placing = (slot[:, None] == jnp.arange(experts * cap, dtype=jnp.int32)[None, :]).astype(
        jnp.bfloat16
    )
    picked = jnp.dot(placing, back.reshape(experts * cap, -1), preferred_element_type=jnp.float32)
    result = (picked * gates[0][:, None]).astype(jnp.bfloat16)
    return result[None, :, :]


def solution(mesh):
    sections, experts = mesh.shape["section"], mesh.shape["expert"]
    x, z = 4, 2
    grid = Mesh(
        mesh.devices.reshape(sections, experts // (x * z), x, z), ("section", "y", "x", "z")
    )
    in_specs = (
        P("section", AXES, None),
        P("section", AXES),
        P("section", AXES, None),
        P("section", AXES),
        P("section", AXES),
        P("section", AXES, None),
        P("section", AXES, None),
        P("section", AXES, None),
        P("section", AXES, None),
        P("section", AXES, None, None),
    )
    out_specs = P("section", AXES, None)
    return jax.shard_map(shards, mesh=grid, in_specs=in_specs, out_specs=out_specs, check_vma=False)
```

```python
import jax
import jax.numpy as jnp
from jax import lax
from jax.experimental import pallas as pl
from jax.experimental.pallas import tpu as pltpu
from jax.sharding import Mesh, PartitionSpec as P

HEADS = 16
EMPTY = 1e30
AXES = ("y", "x", "z")
VMEM = pl.BlockSpec(memory_space=pltpu.VMEM)
SMEM = pl.BlockSpec(memory_space=pltpu.SMEM)
PARAMS = pltpu.CompilerParams(vmem_limit_bytes=20 << 20)
SMALL = pltpu.CompilerParams(vmem_limit_bytes=4 << 20)


def widen_kernel(*refs):
    *pieces, out, sems = refs
    copies = []
    for i in range(out.shape[0]):
        for k, piece in enumerate(pieces):
            to = out.at[i, k] if len(pieces) > 1 else out.at[i]
            copies.append(pltpu.make_async_copy(piece, to, sems.at[i, k]))
    for copy in copies:
        copy.start()
    for copy in copies:
        copy.wait()


def widened(pieces, axis):
    peers, first = lax.axis_size(axis), pieces[0]
    inner = (len(pieces), *first.shape) if len(pieces) > 1 else first.shape
    return pl.pallas_call(
        widen_kernel,
        out_shape=jax.ShapeDtypeStruct((peers, *inner), first.dtype),
        in_specs=[pl.BlockSpec(memory_space=pl.ANY)] * len(pieces),
        out_specs=pl.BlockSpec(memory_space=pltpu.HBM),
        scratch_shapes=[pltpu.SemaphoreType.DMA((peers, len(pieces)))],
        compiler_params=SMALL,
        cost_estimate=pl.CostEstimate(
            flops=0, transcendentals=0, bytes_accessed=4 * peers * len(pieces) * first.size
        ),
        name="widen",
    )(*pieces)


def gathered(pieces, axis):
    return lax.all_to_all(widened(pieces, axis), axis, 0, 0, tiled=True)


def whole(mine, other, low, which):
    first = jnp.where(low, mine[:, :, which], other[:, :, which])
    second = jnp.where(low, other[:, :, which], mine[:, :, which])
    both = jnp.stack([first, second], axis=2)
    return jnp.swapaxes(both, 0, 1).reshape(-1, mine.shape[-1])


def decode_kernel(
    facts, tokens, keys_far, keys_near, values_far, values_near, other, slot, stored, out,
    query, context, mine, sems
):
    decoding, length, low = facts[0] > 0, facts[1], facts[2] > 0
    loading = [
        pltpu.make_async_copy(stored.at[:, :, k], mine.at[:, :, k], sems.at[k]) for k in range(2)
    ]
    loading[0].start()
    loading[1].start()
    own = tokens[...]
    rows, width = own.shape
    slab = 128
    loading[0].wait()
    dim = width // HEADS
    query[...] = jnp.dot(
        own, whole(mine, other, low, 0), preferred_element_type=jnp.float32
    ).astype(jnp.bfloat16)
    span = keys_far.shape[0] + keys_near.shape[0]
    valid = lax.broadcasted_iota(jnp.int32, (rows, span), 1) < length
    lane = lax.broadcasted_iota(jnp.int32, (rows, slab), 1)
    for p in range(width // slab):
        part = slice(p * slab, (p + 1) * slab)
        keys = jnp.concatenate([keys_far[:, part], keys_near[:, part]], axis=0)
        values = jnp.concatenate([values_far[:, part], values_near[:, part]], axis=0)
        pair = query[:, part]
        found = jnp.zeros((rows, slab), jnp.float32)
        for h in range(slab // dim):
            here = (lane >= h * dim) & (lane < (h + 1) * dim)
            asked = jnp.where(here, pair, jnp.zeros_like(pair))
            scores = lax.dot_general(
                asked, keys, (((1,), (1,)), ((), ())), preferred_element_type=jnp.float32
            ) * (dim**-0.5)
            scores = jnp.where(valid, scores, -1e30)
            weights = jnp.exp(scores - jnp.max(scores, axis=1, keepdims=True))
            probs = weights * (1.0 / jnp.sum(weights, axis=1, keepdims=True))
            seen = jnp.dot(probs.astype(jnp.bfloat16), values, preferred_element_type=jnp.float32)
            found = jnp.where(here, seen, found)
        context[:, part] = found.astype(jnp.bfloat16)
    loading[1].wait()
    total = jnp.dot(
        context[...], whole(mine, other, low, 1), preferred_element_type=jnp.float32
    )
    added = (own.astype(jnp.float32) + total).astype(jnp.bfloat16)
    mixed = jnp.where(decoding, added, own)
    slots = out.shape[0]
    index = lax.broadcasted_iota(jnp.int32, (slots, rows), 0)
    placed = (index == slot[...]).astype(jnp.float32)
    used = jnp.sum(placed, axis=1, keepdims=True) > 0.5
    sent = jnp.dot(placed.astype(jnp.bfloat16), mixed, preferred_element_type=jnp.float32)
    out[...] = jnp.where(used, sent, EMPTY).astype(jnp.bfloat16)


def fetch_kernel(stored, held, sem):
    copy = pltpu.make_async_copy(stored.at[:, 0 : held.shape[1]], held, sem)
    copy.start()
    copy.wait()


def expert_kernel(capacity, received, first, stored, out, rest, acts, sems):
    rows, units = acts.shape
    cut = first.shape[1]
    loading = pltpu.make_async_copy(stored.at[:, cut:units], rest, sems.at[0])
    loading.start()
    filled = received[:, 0:128].astype(jnp.float32)[:, 0:1] < EMPTY / 2
    later = lax.broadcasted_iota(jnp.int32, (rows, rows), 0)
    sooner = lax.broadcasted_iota(jnp.int32, (rows, rows), 1)
    before = (sooner < later).astype(jnp.float32).astype(jnp.bfloat16)
    ones = jnp.where(jnp.broadcast_to(filled, (rows, 128)), 1.0, 0.0).astype(jnp.bfloat16)
    rank = jnp.dot(before, ones, preferred_element_type=jnp.float32)[:, 0:1]
    kept = filled & (rank < capacity[0].astype(jnp.float32))
    middle = cut // 256 * 128
    parts = [(0, first, 0, middle), (0, first, middle, cut), (cut, rest, 0, units - cut)]
    storing = []
    for k, (base, weight, low, high) in enumerate(parts):
        part = slice(base + low, base + high)
        if weight is rest:
            loading.wait()
        hidden = jnp.dot(received[...], weight[:, low:high], preferred_element_type=jnp.float32)
        acts[:, part] = jnp.where(kept, jnp.maximum(hidden, 0.0), 0.0).astype(jnp.bfloat16)
        storing.append(pltpu.make_async_copy(acts.at[:, part], out.at[:, part], sems.at[1 + k]))
        storing[k].start()
    for copy in storing:
        copy.wait()


def shards(
    tokens, gates, routes, capacity, mem_lengths, mem_keys, mem_values, q_weight, out_weight, w_in
):
    sections = lax.axis_size("section")
    half = sections // 2
    step = half // 2
    experts = lax.axis_size(AXES)
    inputs = tokens[0]
    tok_dev, width = inputs.shape
    cap = max(8, 2 * tok_dev // experts)

    across = [(s, s + half) for s in range(half)]
    keys_far = lax.ppermute(mem_keys[0], "section", across)
    values_far = lax.ppermute(mem_values[0], "section", across)

    spread = gathered(
        [pltpu.with_memory_space_constraint(w[0], pltpu.HBM) for w in (q_weight, out_weight)], "y"
    )
    beside = lax.ppermute(spread, "z", [(0, 1), (1, 0)])
    beside = widened([beside], "x")
    mine = gathered([spread], "x")
    mine, beside, keys_far = lax.optimization_barrier((mine, beside, keys_far))
    other = lax.all_to_all(beside, "x", 0, 0, tiled=True)
    mine, other, values_far = lax.optimization_barrier((mine, other, values_far))

    route = routes[0, :, 0]
    same = route[:, None] == route[None, :]
    earlier = jnp.arange(tok_dev)[None, :] < jnp.arange(tok_dev)[:, None]
    lrank = jnp.sum((same & earlier).astype(jnp.int32), axis=1)
    slot = route * cap + lrank
    decoding = (lax.axis_index("section") >= half).astype(jnp.int32)

    low = (lax.axis_index("z") == 0).astype(jnp.int32)
    facts = jnp.stack([decoding, mem_lengths[0, 0], low])
    buffer = pl.pallas_call(
        decode_kernel,
        out_shape=jax.ShapeDtypeStruct((experts * cap, width), jnp.bfloat16),
        in_specs=[SMEM] + [VMEM] * 7 + [pl.BlockSpec(memory_space=pltpu.HBM)],
        out_specs=VMEM,
        scratch_shapes=[pltpu.VMEM((tok_dev, width), jnp.bfloat16)] * 2
        + [pltpu.VMEM(mine.shape, jnp.bfloat16), pltpu.SemaphoreType.DMA((2,))],
        compiler_params=pltpu.CompilerParams(vmem_limit_bytes=32 << 20),
        name="decode",
    )(
        facts,
        inputs,
        keys_far,
        mem_keys[0],
        values_far,
        mem_values[0],
        other,
        slot[None, :],
        pltpu.with_memory_space_constraint(mine, pltpu.HBM),
    )
    received = lax.all_to_all(
        buffer.reshape(experts, cap, width), AXES, split_axis=0, concat_axis=0, tiled=True
    )
    units = w_in.shape[-1]
    cut = units // 512 * 512
    stored = pltpu.with_memory_space_constraint(w_in[0, 0], pltpu.HBM)
    first = pl.pallas_call(
        fetch_kernel,
        out_shape=jax.ShapeDtypeStruct((width, cut), jnp.bfloat16),
        in_specs=[pl.BlockSpec(memory_space=pltpu.HBM)],
        out_specs=VMEM,
        scratch_shapes=[pltpu.SemaphoreType.DMA(())],
        compiler_params=SMALL,
        name="fetch",
    )(stored)
    acts = pl.pallas_call(
        expert_kernel,
        out_shape=pltpu.HBM((experts * cap, units), jnp.bfloat16),
        in_specs=[SMEM, VMEM, VMEM, pl.BlockSpec(memory_space=pltpu.HBM)],
        out_specs=pl.BlockSpec(memory_space=pltpu.HBM),
        scratch_shapes=[
            pltpu.VMEM((width, units - cut), jnp.bfloat16),
            pltpu.VMEM((experts * cap, units), jnp.bfloat16),
            pltpu.SemaphoreType.DMA((4,)),
        ],
        compiler_params=PARAMS,
        name="expert",
    )(capacity[0], received.reshape(experts * cap, width), first, stored)
    back = lax.all_to_all(
        acts.reshape(experts, cap, -1), AXES, split_axis=0, concat_axis=0, tiled=True
    )
    placing = (slot[:, None] == jnp.arange(experts * cap, dtype=jnp.int32)[None, :]).astype(
        jnp.bfloat16
    )
    picked = jnp.dot(placing, back.reshape(experts * cap, -1), preferred_element_type=jnp.float32)
    result = (picked * gates[0][:, None]).astype(jnp.bfloat16)
    return result[None, :, :]


def solution(mesh):
    sections, experts = mesh.shape["section"], mesh.shape["expert"]
    x, z = 4, 2
    grid = Mesh(
        mesh.devices.reshape(sections, experts // (x * z), x, z), ("section", "y", "x", "z")
    )
    in_specs = (
        P("section", AXES, None),
        P("section", AXES),
        P("section", AXES, None),
        P("section", AXES),
        P("section", AXES),
        P("section", AXES, None),
        P("section", AXES, None),
        P("section", AXES, None),
        P("section", AXES, None),
        P("section", AXES, None, None),
    )
    out_specs = P("section", AXES, None)
    return jax.shard_map(shards, mesh=grid, in_specs=in_specs, out_specs=out_specs, check_vma=False)
```
